256 devices in a mesh: elem: 16 (over z, y_hi), orb: 16 (over x, y_lo, core).
Axes of the slice: x: 4, y: 4 (y_hi: 2, y_lo: 2; y = y_hi * 2 + y_lo), z: 8, core: 2. Of those that a mesh axis runs over, the one named last changes fastest.
Arguments:
- hamiltonian: bfloat16 [512, 7, 128, 128], P('elem'), may hold values from -1 to 1, as said below
- start: bfloat16 [512, 128, 1024], P('elem', None, 'orb'), may hold values from -6 to 6
- ritz: bfloat16 [1024, 1024], P(None, 'orb'), may hold values from -0.1875 to 0.1875
Outputs:
- margin: float32 [1024, 1024], P('orb', 'elem')
- rotated: float32 [512, 128, 1024], P('elem', None, 'orb')
The draws below stay inside these ranges and needn't reach their ends.
Inputs may be any that keep to these rules, and one draw needn't show every extreme that they name: hamiltonian[e, 1 + 2 k] is the transpose of hamiltonian[n(e, 1 + 2 k), 2 + 2 k], and each diagonal block hamiltonian[e, 0] is symmetric, so the operator is symmetric.
All inputs are finite; a program needn't handle non-finite values.
Results may differ from the reference program's by a relative error of at most 0.0095.
Values may be sent and summed in bfloat16 or wider, within the bound.
No kernel may reach another device: no remote copies, remote signals or barrier semaphores. Data moves between devices by JAX's collectives and lax.ppermute only.
A program may use at most 64 MiB of HBM per device.

```python
import math
import jax
import jax.numpy as jnp

NB = 128
NORB = 1024
GY = 4
GZ = 4
DEG = 6
GX = 32
E = 512
ROWS = 65536


def draw_hamiltonian(key, part):
    key_forward = jax.random.fold_in(key, 11)
    key_self = jax.random.fold_in(key, 12)
    key_potential = jax.random.fold_in(key, 13)
    block_scale = 0.5 / math.sqrt(7.0 * NB)
    forward = jnp.clip(jax.random.normal(key_forward, (GX, GY, GZ, 3, NB, NB), jnp.float32), -4.0, 4.0)
    raw_self = jnp.clip(jax.random.normal(key_self, (GX, GY, GZ, NB, NB), jnp.float32), -4.0, 4.0)
    forward = forward * block_scale
    potential = jax.random.uniform(key_potential, (GX, GY, GZ, NB), jnp.float32, -0.3, 0.3)
    eye_table = jnp.eye(NB, dtype=jnp.float32)
    self_block = (raw_self + jnp.swapaxes(raw_self, -1, -2)) * (block_scale / math.sqrt(2.0)) + potential[..., :, None] * eye_table
    minus_x = jnp.swapaxes(jnp.roll(forward[:, :, :, 0], 1, axis=0), -1, -2)
    minus_y = jnp.swapaxes(jnp.roll(forward[:, :, :, 1], 1, axis=1), -1, -2)
    minus_z = jnp.swapaxes(jnp.roll(forward[:, :, :, 2], 1, axis=2), -1, -2)
    stacked = jnp.stack([self_block, minus_x, forward[:, :, :, 0], minus_y, forward[:, :, :, 1], minus_z, forward[:, :, :, 2]], axis=3)
    return stacked.reshape(GX * GY * GZ, 7, NB, NB).astype(jnp.bfloat16)


def steps_of(stream_key, extent, split, low, high):
    gain = 1.0
    for dim, shards_of in split:
        heights = jax.random.uniform(jax.random.fold_in(jax.random.fold_in(stream_key, 6), dim), (shards_of,), jnp.float32, low / len(split), high / len(split))
        gain = gain * jnp.repeat(jnp.exp(heights), extent[dim] // shards_of).reshape((-1,) + (1,) * (len(extent) - 1 - dim))
    return gain


def gaussian(stream_key, extent, deviation, limit, shards=(), held_as=jnp.bfloat16):
    level = steps_of(stream_key, extent, shards, -0.22, 0.18) if shards else 1.0
    array = jax.random.normal(stream_key, extent, jnp.float32) * deviation * level
    return jnp.minimum(jnp.maximum(array, -limit), limit).astype(held_as)


def setup_inputs(seed: int = 0) -> dict:
    splits = jax.random.split(jax.random.key(seed), 4)
    return {
        "hamiltonian": draw_hamiltonian(jax.random.fold_in(splits[3], 71), 0),
        "start": gaussian(splits[1], (E, NB, NORB), 1.0, 6.0, ((0, 16), (2, 16))),
        "ritz": gaussian(splits[2], (NORB, NORB), NORB ** -0.5, 0.1875, ((1, 16),)),
    }


center_shift = 0.1
half_width = 1.25


def apply_ham(hamiltonian, rounded):
    element_grid = rounded.reshape(GX, GY, GZ, NB, NORB)
    neighbours = [element_grid,
                  jnp.roll(element_grid, 1, axis=0), jnp.roll(element_grid, -1, axis=0),
                  jnp.roll(element_grid, 1, axis=1), jnp.roll(element_grid, -1, axis=1),
                  jnp.roll(element_grid, 1, axis=2), jnp.roll(element_grid, -1, axis=2)]
    accumulated = jnp.zeros((E, NB, NORB), jnp.float32)
    for direction in range(7):
        block_set = hamiltonian[:, direction].astype(jnp.float32)
        moved = neighbours[direction].reshape(E, NB, NORB).astype(jnp.float32)
        accumulated = accumulated + jnp.einsum('eij,ejo->eio', block_set, moved)
    return accumulated


def reference(hamiltonian, start, ritz):
    previous = start.astype(jnp.float32)
    current = (apply_ham(hamiltonian, start) - center_shift * previous) / half_width
    for degree in range(DEG - 1):
        rounded = current.astype(jnp.bfloat16)
        image = apply_ham(hamiltonian, rounded)
        following = (2.0 / half_width) * (image - center_shift * current) - previous
        previous = current
        current = following
    filtered = current.astype(jnp.bfloat16).reshape(ROWS, NORB)
    margin = jnp.dot(filtered.T, filtered, preferred_element_type=jnp.float32) / float(ROWS)
    rotated = jnp.dot(filtered, ritz, preferred_element_type=jnp.float32).reshape(E, NB, NORB)
    return margin, rotated
```

```python
import jax
import jax.numpy as jnp
from jax import lax
from jax.sharding import Mesh, PartitionSpec as P

GY = 4
GZ = 4
NB = 128
DEG = 6
PLANE = GY * GZ

center_shift = 0.1
half_width = 1.25

ELEM = ("z", "yh")
ORB = ("x", "yl", "c")
CHIP = ("x", "yl")


def blocks(ham, direction, values):
    return jnp.einsum("eij,eoj->eoi", ham[:, direction], values, preferred_element_type=jnp.float32)


def rolled(values, axis, shift):
    grid = values.reshape(GY, GZ, values.shape[1], NB)
    return jnp.roll(grid, shift, axis=axis).reshape(values.shape)


def interior(ham, own, inner, inner_direction):
    total = blocks(ham, 0, own) + blocks(ham, inner_direction, inner)
    total = total + blocks(ham, 3, rolled(own, 0, 1)) + blocks(ham, 4, rolled(own, 0, -1))
    return total + blocks(ham, 5, rolled(own, 1, 1)) + blocks(ham, 6, rolled(own, 1, -1))


def recur(image, current, previous, first):
    if first:
        return (image - center_shift * current) / half_width
    return 2.0 / half_width * (image - center_shift * current) - previous


def on_device(hamiltonian, start, ritz):
    slabs = lax.axis_size("z") * lax.axis_size("yh")
    chips = lax.axis_size("x") * lax.axis_size("yl")
    rows_total = float(slabs * hamiltonian.shape[0] * NB)
    orb_cols = start.shape[2]
    up = [(i, (i + 1) % slabs) for i in range(slabs)]
    down = [((i + 1) % slabs, i) for i in range(slabs)]
    ham_a, ham_b = hamiltonian[:PLANE], hamiltonian[PLANE:]
    begin = jnp.swapaxes(start, 1, 2)
    a, b = begin[:PLANE], begin[PLANE:]
    left = lax.ppermute(b, ELEM, up)
    right = lax.ppermute(a, ELEM, down)
    ritz_rows = jnp.swapaxes(ritz, 0, 1)
    ritz_chip = lax.all_to_all(
        jnp.broadcast_to(ritz_rows, (chips,) + ritz_rows.shape), CHIP, 0, 0, tiled=False
    )
    cur_a, cur_b = a.astype(jnp.float32), b.astype(jnp.float32)
    prev_a = prev_b = None
    for k in range(DEG):
        last = k == DEG - 1
        part_a = interior(ham_a, a, b, 2)
        image_a = part_a + blocks(ham_a, 1, left)
        next_a = recur(image_a, cur_a, prev_a, k == 0)
        new_a = next_a.astype(jnp.bfloat16)
        if not last:
            new_right = lax.ppermute(new_a, ELEM, down)
        b_held, _ = lax.optimization_barrier((b, new_a))
        part_b = interior(ham_b, b_held, a, 1)
        image_b = part_b + blocks(ham_b, 2, right)
        next_b = recur(image_b, cur_b, prev_b, k == 0)
        new_b = next_b.astype(jnp.bfloat16)
        if not last:
            left = lax.ppermute(new_b, ELEM, up)
            right = new_right
        prev_a, cur_a, a = cur_a, next_a, new_a
        prev_b, cur_b, b = cur_b, next_b, new_b
    filtered = jnp.concatenate([a, b], axis=0)

    mine = lax.all_to_all(filtered, CHIP, 0, 0, tiled=True)
    other = lax.ppermute(mine, "c", [(0, 1), (1, 0)])
    core = lax.axis_index("c")
    held = mine.shape[0] // chips
    shape = (chips, held, orb_cols, NB)
    mine, other = mine.reshape(shape), other.reshape(shape)
    first = core == 0
    everyone = jnp.stack([jnp.where(first, mine, other), jnp.where(first, other, mine)], axis=1)
    part = jnp.einsum("seib,tcejb->sitcj", mine, everyone, preferred_element_type=jnp.float32)
    part = part.astype(jnp.bfloat16).reshape(chips, orb_cols, chips * 2 * orb_cols)
    ritz_chip = ritz_chip.reshape(chips, orb_cols, chips, 2, orb_cols)
    turned = jnp.einsum("dktcj,tcejb->dekb", ritz_chip, everyone, preferred_element_type=jnp.float32)
    part = lax.all_to_all(part, CHIP, 0, 0, tiled=True)
    turned = lax.all_to_all(turned.astype(jnp.bfloat16), CHIP, 0, 0, tiled=True)
    margin_rows = jnp.sum(part.astype(jnp.float32), axis=0).astype(jnp.bfloat16)
    half = orb_cols // 2
    margin_rows = margin_rows.reshape(2, half, slabs, orb_cols).transpose(2, 1, 0, 3)
    margin_rows = margin_rows.reshape(slabs, half, 2 * orb_cols)
    margin_rows = lax.all_to_all(margin_rows, ELEM, 0, 0, tiled=True)
    margin = jnp.sum(margin_rows.astype(jnp.float32), axis=0) / rows_total
    margin = margin.reshape(half, 2, orb_cols).transpose(1, 0, 2).reshape(orb_cols, orb_cols)
    rotated = turned.reshape(chips * held, orb_cols, NB).astype(jnp.float32)
    return margin, jnp.swapaxes(rotated, 1, 2)


def solution(mesh):
    fine = Mesh(mesh.devices.reshape(8, 2, 4, 2, 2), ("z", "yh", "x", "yl", "c"))
    in_specs = (P(ELEM, None, None, None), P(ELEM, None, ORB), P(None, ORB))
    out_specs = (P(ORB, ELEM), P(ELEM, None, ORB))
    return jax.shard_map(on_device, mesh=fine, in_specs=in_specs, out_specs=out_specs, check_vma=False)
```

```python
import functools

import jax
import jax.numpy as jnp
from jax import lax
from jax.experimental import pallas as pl
from jax.experimental.pallas import tpu as pltpu
from jax.sharding import Mesh, PartitionSpec as P


GY = 4
GZ = 4
NB = 128
DEG = 6
PLANE = GY * GZ

center_shift = 0.1
half_width = 1.25

ELEM = ("z", "yh")
ORB = ("x", "yl", "c")
CHIP = ("x", "yl")
VMEM = pl.BlockSpec(memory_space=pltpu.VMEM)


def weighted(ham, e, pair):
    return jnp.concatenate([ham[e, d] for d in pair], axis=1)


def interior_kernel(base, inside, scale, shift, has_previous, ham, own, inner, current, *rest):
    previous, out = rest if has_previous else (None, rest[0])
    contract = (((1,), (1,)), ((), ()))

    def plane(gy, carry):
        above = lax.rem(gy + GY - 1, GY) * GZ
        below = lax.rem(gy + 1, GY) * GZ
        for gz in range(GZ):
            e = gy * GZ + gz
            values = {
                0: own[e],
                inside: inner[e],
                3: own[above + gz],
                4: own[below + gz],
                5: own[gy * GZ + (gz - 1) % GZ],
                6: own[gy * GZ + (gz + 1) % GZ],
            }
            total = None
            for pair in ((0, inside), (3, 4), (5, 6)):
                left = jnp.concatenate([values[d] for d in pair], axis=1)
                term = lax.dot_general(left, weighted(ham, base + e, pair), contract, preferred_element_type=jnp.float32)
                total = term if total is None else total + term
            total = scale * total - shift * current[e].astype(jnp.float32)
            if has_previous:
                total = total - previous[e].astype(jnp.float32)
            out[e] = total
        return carry

    lax.fori_loop(0, GY, plane, 0)


def boundary_kernel(base, direction, scale, ham, halo, partial, full, rounded):
    contract = (((1,), (1,)), ((), ()))

    def plane(gy, carry):
        for gz in range(GZ):
            e = gy * GZ + gz
            term = lax.dot_general(halo[e], ham[base + e, direction], contract, preferred_element_type=jnp.float32)
            value = partial[e] + scale * term
            full[e] = value
            rounded[e] = value.astype(jnp.bfloat16)
        return carry

    lax.fori_loop(0, GY, plane, 0)


def cost(elements, cols, directions):
    size = elements * cols * NB
    return pl.CostEstimate(flops=2 * size * NB * directions, bytes_accessed=elements * NB * NB * 2 * directions, transcendentals=0)


def interior(ham, base, own, inner, inside, current, previous):
    first = previous is None
    scale = (1.0 if first else 2.0) / half_width
    operands = [ham, own, inner, current] + ([] if first else [previous])
    return pl.pallas_call(
        functools.partial(interior_kernel, base, inside, scale, scale * center_shift, not first),
        out_shape=jax.ShapeDtypeStruct(own.shape, jnp.float32),
        in_specs=[VMEM] * len(operands),
        out_specs=VMEM,
        cost_estimate=cost(own.shape[0], own.shape[1], 6),
        compiler_params=pltpu.CompilerParams(vmem_limit_bytes=12 << 20),
    )(*operands)


def boundary(ham, base, outside, halo, partial, first):
    scale = (1.0 if first else 2.0) / half_width
    return pl.pallas_call(
        functools.partial(boundary_kernel, base, outside, scale),
        out_shape=(
            jax.ShapeDtypeStruct(partial.shape, jnp.float32),
            jax.ShapeDtypeStruct(partial.shape, jnp.bfloat16),
        ),
        in_specs=[VMEM] * 3,
        out_specs=(VMEM, VMEM),
        cost_estimate=cost(halo.shape[0], halo.shape[1], 1),
        compiler_params=pltpu.CompilerParams(vmem_limit_bytes=12 << 20),
    )(ham, halo, partial)


def message_kernel(chips, core_ref, mine0, mine1, other0, other1, ritz, out, rows, own):
    cols = mine0.shape[2]
    held = mine0.shape[1]

    def fill(parity, source0, source1):
        for t in range(chips):
            for layer, source in enumerate((source0, source1)):
                for el in range(held):
                    at = (layer * held + el) * NB
                    rows[pl.ds((2 * t + parity) * cols, cols), pl.ds(at, NB)] = source[t, el]

    for t in range(chips):
        for layer, source in enumerate((mine0, mine1)):
            for el in range(held):
                own[pl.ds(t * cols, cols), pl.ds((layer * held + el) * NB, NB)] = source[t, el]

    @pl.when(core_ref[0] == 0)
    def _():
        fill(0, mine0, mine1)
        fill(1, other0, other1)

    @pl.when(core_ref[0] != 0)
    def _():
        fill(1, mine0, mine1)
        fill(0, other0, other1)

    contract = (((1,), (1,)), ((), ()))
    plain = (((1,), (0,)), ((), ()))
    base = chips * cols
    for s in range(0, chips, 2):
        left = own[pl.ds(s * cols, 2 * cols), :]
        part = lax.dot_general(left, rows[...], contract, preferred_element_type=jnp.float32)
        part = part.astype(jnp.bfloat16)
        for q in range(2):
            for t in range(chips):
                out[s + q, pl.ds(t * cols, cols), :] = part[q * cols : (q + 1) * cols, t * NB : (t + 1) * NB]
    for d in range(0, chips, 2):
        left = ritz[pl.ds(d * cols, 2 * cols), :]
        turned = lax.dot_general(left, rows[...], plain, preferred_element_type=jnp.float32)
        turned = turned.astype(jnp.bfloat16)
        for q in range(2):
            for el in range(2 * held):
                out[d + q, pl.ds(base + el * cols, cols), :] = turned[q * cols : (q + 1) * cols, el * NB : (el + 1) * NB]


def message(core, mine0, mine1, other0, other1, ritz):
    chips, held, cols, _ = mine0.shape
    depth = 2 * held * NB
    flops = 2 * (chips * cols) * (2 * chips * cols) * depth * 2
    return pl.pallas_call(
        functools.partial(message_kernel, chips),
        out_shape=jax.ShapeDtypeStruct((chips, (chips + 2 * held) * cols, NB), jnp.bfloat16),
        in_specs=[pl.BlockSpec(memory_space=pltpu.SMEM)] + [VMEM] * 5,
        out_specs=VMEM,
        scratch_shapes=[
            pltpu.VMEM((2 * chips * cols, depth), jnp.bfloat16),
            pltpu.VMEM((chips * cols, depth), jnp.bfloat16),
        ],
        cost_estimate=pl.CostEstimate(flops=flops, bytes_accessed=4 << 20, transcendentals=0),
        compiler_params=pltpu.CompilerParams(vmem_limit_bytes=24 << 20),
        name="message",
    )(core, mine0, mine1, other0, other1, ritz)


def step(hamiltonian, start, ritz):
    slabs = lax.axis_size("z") * lax.axis_size("yh")
    chips = lax.axis_size("x") * lax.axis_size("yl")
    rows_total = float(slabs * hamiltonian.shape[0] * NB)
    orb_cols = start.shape[2]
    up = [(i, (i + 1) % slabs) for i in range(slabs)]
    down = [((i + 1) % slabs, i) for i in range(slabs)]
    begin = jnp.swapaxes(start, 1, 2)
    base = {"a": 0, "b": PLANE}
    val = {("a", 0): begin[:PLANE], ("b", 0): begin[PLANE:]}
    full = dict(val)
    halo = {}

    def send(name, k):
        if name == "a":
            halo["b", k] = lax.ppermute(val["a", k], ELEM, down)
        else:
            halo["a", k] = lax.ppermute(val["b", k], ELEM, up)

    send("b", 0)
    send("a", 0)
    ritz_rows = jnp.swapaxes(ritz, 0, 1)
    ritz_chip = lax.all_to_all(
        jnp.broadcast_to(ritz_rows, (chips,) + ritz_rows.shape), CHIP, 0, 0, tiled=False
    )

    order = []
    for k in range(1, DEG + 1):
        order += [("a", k), ("b", k)] if k % 2 else [("b", k), ("a", k)]
    token = None
    rows = {}
    for count, (name, k) in enumerate(order):
        other = "b" if name == "a" else "a"
        inside, outside = (2, 1) if name == "a" else (1, 2)
        own, inner = val[name, k - 1], val[other, k - 1]
        if token is not None:
            own, inner, _ = lax.optimization_barrier((own, inner, token))
        part = interior(hamiltonian, base[name], own, inner, inside, full[name, k - 1], full.get((name, k - 2)))
        if count == 2 * DEG - 1:
            done, part, ritz_chip = lax.optimization_barrier((val[other, k], part, ritz_chip))
            rows[other] = lax.all_to_all(done, CHIP, 0, 0, tiled=True)
            edge = hamiltonian[base[name] : base[name] + PLANE, outside : outside + 1]
            full[name, k], token = boundary(edge, 0, 0, halo[name, k - 1], part, k == 1)
            rows[name] = lax.all_to_all(token, CHIP, 0, 0, tiled=True)
        else:
            full[name, k], token = boundary(hamiltonian, base[name], outside, halo[name, k - 1], part, k == 1)
        val[name, k] = token
        if k < DEG:
            send(name, k)
    rows = {n: r.reshape(chips, PLANE // chips, orb_cols, NB) for n, r in rows.items()}
    swap = {n: lax.ppermute(r, "c", [(0, 1), (1, 0)]) for n, r in rows.items()}

    core = lax.axis_index("c").astype(jnp.int32).reshape(1)
    sent = message(core, rows["a"], rows["b"], swap["a"], swap["b"], ritz_chip.reshape(chips * orb_cols, -1))
    got = lax.all_to_all(sent, CHIP, 0, 0, tiled=True)
    part, turned = got[:, : chips * orb_cols], got[:, chips * orb_cols :]
    total = jnp.sum(part.astype(jnp.float32), axis=0).astype(jnp.bfloat16)
    half = orb_cols // 2
    total = total.reshape(chips, 2, half, 2, orb_cols).transpose(0, 3, 2, 1, 4)
    total = lax.all_to_all(total.reshape(slabs, half, 2 * orb_cols), ELEM, 0, 0, tiled=True)
    margin = jnp.sum(total.astype(jnp.float32), axis=0) / rows_total
    margin = margin.reshape(half, 2, orb_cols).transpose(1, 0, 2).reshape(orb_cols, orb_cols)
    turned = turned.reshape(chips, 2, PLANE // chips, orb_cols, NB).transpose(1, 0, 2, 3, 4)
    rotated = turned.reshape(2 * PLANE, orb_cols, NB).astype(jnp.float32)
    return margin, jnp.swapaxes(rotated, 1, 2)


def solution(mesh):
    fine = Mesh(mesh.devices.reshape(8, 2, 4, 2, 2), ("z", "yh", "x", "yl", "c"))
    in_specs = (P(ELEM, None, None, None), P(ELEM, None, ORB), P(None, ORB))
    out_specs = (P(ORB, ELEM), P(ELEM, None, ORB))
    return jax.shard_map(step, mesh=fine, in_specs=in_specs, out_specs=out_specs, check_vma=False)
```

```python
import functools

import jax
import jax.numpy as jnp
from jax import lax
from jax.experimental import pallas as pl
from jax.experimental.pallas import tpu as pltpu
from jax.sharding import Mesh, PartitionSpec as P


GY = 4
GZ = 4
NB = 128
DEG = 6
PLANE = GY * GZ

center_shift = 0.1
half_width = 1.25

ELEM = ("z", "yh")
ORB = ("x", "yl", "c")
CHIP = ("x", "yl")
VMEM = pl.BlockSpec(memory_space=pltpu.VMEM)
SMEM = pl.BlockSpec(memory_space=pltpu.SMEM)
ROWS = (((1,), (1,)), ((), ()))
PLAIN = (((1,), (0,)), ((), ()))


def product(left, right, contract):
    return lax.dot_general(left, right, contract, preferred_element_type=jnp.float32)


def inside_kernel(base, inside, scale, shift, has_previous, ham, own, inner, current, *rest):
    previous, out = rest if has_previous else (None, rest[0])

    def line(gy, carry):
        above = lax.rem(gy + GY - 1, GY) * GZ
        below = lax.rem(gy + 1, GY) * GZ
        for gz in range(GZ):
            e = gy * GZ + gz
            values = {
                0: own[e],
                inside: inner[e],
                3: own[above + gz],
                4: own[below + gz],
                5: own[gy * GZ + (gz - 1) % GZ],
                6: own[gy * GZ + (gz + 1) % GZ],
            }
            total = None
            for pair in ((0, inside), (3, 4), (5, 6)):
                left = jnp.concatenate([values[d] for d in pair], axis=1)
                right = jnp.concatenate([ham[base + e, d] for d in pair], axis=1)
                term = product(left, right, ROWS)
                total = term if total is None else total + term
            total = scale * total - shift * current[e].astype(jnp.float32)
            if has_previous:
                total = total - previous[e].astype(jnp.float32)
            out[e] = total
        return carry

    lax.fori_loop(0, GY, line, 0)


def outside_kernel(base, direction, scale, ham, halo, partial, rounded, *full):
    def line(gy, carry):
        for gz in range(GZ):
            e = gy * GZ + gz
            value = partial[e] + scale * product(halo[e], ham[base + e, direction], ROWS)
            rounded[e] = value.astype(jnp.bfloat16)
            if full:
                full[0][e] = value
        return carry

    lax.fori_loop(0, GY, line, 0)


def last_kernel(base, direction, scale, ham, halo, partial, other, filtered):
    def line(gy, carry):
        for gz in range(GZ):
            e = gy * GZ + gz
            value = partial[e] + scale * product(halo[e], ham[base + e, direction], ROWS)
            filtered[base + e] = value.astype(jnp.bfloat16)
            filtered[PLANE - base + e] = other[e]
        return carry

    lax.fori_loop(0, GY, line, 0)


def cost(elements, cols, directions):
    size = elements * cols * NB
    read = elements * NB * NB * 2 * directions
    return pl.CostEstimate(flops=2 * size * NB * directions, bytes_accessed=read, transcendentals=0)


def call(kernel, operands, out_shape, estimate, limit, scratch=(), in_specs=None):
    many = isinstance(out_shape, tuple)
    return pl.pallas_call(
        kernel,
        out_shape=out_shape,
        in_specs=in_specs or [VMEM] * len(operands),
        out_specs=(VMEM,) * len(out_shape) if many else VMEM,
        scratch_shapes=scratch,
        cost_estimate=estimate,
        compiler_params=pltpu.CompilerParams(vmem_limit_bytes=limit << 20),
    )(*operands)


def message_kernel(chips, place, mine, other, ritz, ritz_back, ritz_next, ritz_far, out, rows, own):
    held, cols = mine.shape[1], mine.shape[2]

    def fill(parity, source):
        for t in range(chips):
            for el in range(held):
                rows[pl.ds((2 * t + parity) * cols, cols), pl.ds(el * NB, NB)] = source[t, el]

    for t in range(chips):
        for el in range(held):
            own[pl.ds(t * cols, cols), pl.ds(el * NB, NB)] = mine[t, el]

    @pl.when(place[2] == 0)
    def _():
        fill(0, mine)
        fill(1, other)

    @pl.when(place[2] != 0)
    def _():
        fill(1, mine)
        fill(0, other)

    base = chips * cols
    for s in range(0, chips, 2):
        part = product(own[pl.ds(s * cols, 2 * cols), :], rows[...], ROWS).astype(jnp.bfloat16)
        for q in range(2):
            for t in range(chips):
                out[s + q, pl.ds(t * cols, cols), :] = part[q * cols : (q + 1) * cols, t * NB : (t + 1) * NB]
    around = chips // 2
    for away, source in ((0, ritz), (around - 1, ritz_back), (1, ritz_next), (2, ritz_far)):
        turned = product(source[...].reshape(2 * cols, -1), rows[...], PLAIN).astype(jnp.bfloat16)
        for q in range(2):
            to = lax.rem(place[0] + away, around) * 2 + (place[1] if q == 0 else 1 - place[1])
            for el in range(held):
                piece = turned[q * cols : (q + 1) * cols, el * NB : (el + 1) * NB]
                out[to, pl.ds(base + el * cols, cols), :] = piece


def margin_rows_kernel(chips, got, out):
    cols = out.shape[2] // 2
    half = cols // 2
    for t in range(chips):
        total = got[0, pl.ds(t * cols, cols), :].astype(jnp.float32)
        for s in range(1, chips):
            total = total + got[s, pl.ds(t * cols, cols), :].astype(jnp.float32)
        for core in range(2):
            block = total[:, core * cols : (core + 1) * cols]
            out[2 * t + core] = jnp.concatenate([block[:half], block[half:]], axis=1).astype(jnp.bfloat16)


def margin_kernel(scale, got, out):
    total = got[0].astype(jnp.float32)
    for s in range(1, got.shape[0]):
        total = total + got[s].astype(jnp.float32)
    total = total * scale
    half, cols = got.shape[1], out.shape[1]
    out[0:half, :] = total[:, :cols]
    out[half : 2 * half, :] = total[:, cols:]


def whole(hamiltonian, start, ritz):
    slabs = lax.axis_size("z") * lax.axis_size("yh")
    chips = lax.axis_size("x") * lax.axis_size("yl")
    around = lax.axis_size("x")
    rows_total = float(slabs * hamiltonian.shape[0] * NB)
    cols = start.shape[2]
    layer = jax.ShapeDtypeStruct((PLANE, cols, NB), jnp.float32)
    up = [(i, (i + 1) % slabs) for i in range(slabs)]
    down = [((i + 1) % slabs, i) for i in range(slabs)]
    begin = jnp.swapaxes(start, 1, 2)
    base = {"a": 0, "b": PLANE}
    val = {("a", 0): begin[:PLANE], ("b", 0): begin[PLANE:]}
    full = dict(val)
    halo = {}

    def send(name, k):
        if name == "a":
            halo["b", k] = lax.ppermute(val["a", k], ELEM, down)
        else:
            halo["a", k] = lax.ppermute(val["b", k], ELEM, up)

    send("b", 0)
    send("a", 0)

    order = []
    for k in range(1, DEG + 1):
        order += [("a", k), ("b", k)] if k % 2 else [("b", k), ("a", k)]
    token = None
    shared = {"own": jnp.swapaxes(ritz, 0, 1)}
    for count, (name, k) in enumerate(order):
        other = "b" if name == "a" else "a"
        inside, outside = (2, 1) if name == "a" else (1, 2)
        own, inner = val[name, k - 1], val[other, k - 1]
        if token is not None:
            own, inner, _ = lax.optimization_barrier((own, inner, token))
        scale = (1.0 if k == 1 else 2.0) / half_width
        operands = [hamiltonian, own, inner, full[name, k - 1]]
        if k > 1:
            operands.append(full[name, k - 2])
        part = call(
            functools.partial(inside_kernel, base[name], inside, scale, scale * center_shift, k > 1),
            operands, layer, cost(PLANE, cols, 6), 12,
        )
        edge = [hamiltonian, halo[name, k - 1], part]
        if count == 2 * DEG - 1:
            filtered = call(
                functools.partial(last_kernel, base[name], outside, scale),
                edge + [val[other, k]],
                jax.ShapeDtypeStruct((2 * PLANE, cols, NB), jnp.bfloat16), cost(PLANE, cols, 1), 12,
            )
            break
        kept = (layer,) if k < DEG else ()
        token, *kept = call(
            functools.partial(outside_kernel, base[name], outside, scale),
            edge, (layer.update(dtype=jnp.bfloat16), *kept), cost(PLANE, cols, 1), 12,
        )
        val[name, k] = token
        if kept:
            full[name, k] = kept[0]
        if k < DEG:
            send(name, k)
        if count == 1:
            source, _ = lax.optimization_barrier((shared["own"], token))
            shared["pair"] = jnp.stack([source, lax.ppermute(source, "yl", [(0, 1), (1, 0)])])
        elif count in (4, 6, 8):
            shift = {4: 1, 6: around - 1, 8: 2}[count]
            source, _ = lax.optimization_barrier((shared["pair"], token))
            shared[shift] = lax.ppermute(source, "x", [(i, (i + shift) % around) for i in range(around)])

    mine = lax.all_to_all(filtered, CHIP, 0, 0, tiled=True)
    mine = mine.reshape(chips, 2 * PLANE // chips, cols, NB)
    theirs = lax.ppermute(mine, "c", [(0, 1), (1, 0)])
    place = jnp.stack([lax.axis_index("x"), lax.axis_index("yl"), lax.axis_index("c")]).astype(jnp.int32)
    held = mine.shape[1]
    depth = held * NB
    sent = call(
        functools.partial(message_kernel, chips),
        (place, mine, theirs, shared["pair"], shared[1], shared[around - 1], shared[2]),
        jax.ShapeDtypeStruct((chips, (chips + held) * cols, NB), jnp.bfloat16),
        pl.CostEstimate(flops=8 * (chips * cols) ** 2 * depth, bytes_accessed=4 << 20, transcendentals=0),
        24,
        (pltpu.VMEM((2 * chips * cols, depth), jnp.bfloat16), pltpu.VMEM((chips * cols, depth), jnp.bfloat16)),
        [SMEM] + [VMEM] * 6,
    )
    got = lax.all_to_all(sent, CHIP, 0, 0, tiled=True)
    small = pl.CostEstimate(flops=1 << 20, bytes_accessed=1 << 20, transcendentals=0)
    rows = call(
        functools.partial(margin_rows_kernel, chips), (got,),
        jax.ShapeDtypeStruct((slabs, cols // 2, 2 * cols), jnp.bfloat16), small, 12,
    )
    rows = lax.all_to_all(rows, ELEM, 0, 0, tiled=True)
    margin = call(
        functools.partial(margin_kernel, 1.0 / rows_total), (rows,),
        jax.ShapeDtypeStruct((cols, cols), jnp.float32), small, 12,
    )
    turned = got[:, chips * cols :].reshape(2 * PLANE, cols, NB).astype(jnp.float32)
    return margin, jnp.swapaxes(turned, 1, 2)


def solution(mesh):
    fine = Mesh(mesh.devices.reshape(8, 2, 4, 2, 2), ("z", "yh", "x", "yl", "c"))
    in_specs = (P(ELEM, None, None, None), P(ELEM, None, ORB), P(None, ORB))
    out_specs = (P(ORB, ELEM), P(ELEM, None, ORB))
    return jax.shard_map(whole, mesh=fine, in_specs=in_specs, out_specs=out_specs, check_vma=False)
```

```python
import functools

import jax
import jax.numpy as jnp
from jax import lax
from jax.experimental import pallas as pl
from jax.experimental.pallas import tpu as pltpu
from jax.sharding import Mesh, PartitionSpec as P


GY = 4
GZ = 4
NB = 128
DEG = 6
PLANE = GY * GZ

center_shift = 0.1
half_width = 1.25

ELEM = ("z", "yh")
ORB = ("x", "yl", "c")
CHIP = ("x", "yl")
VMEM = pl.BlockSpec(memory_space=pltpu.VMEM)
SMEM = pl.BlockSpec(memory_space=pltpu.SMEM)
ROWS = (((1,), (1,)), ((), ()))
PLAIN = (((1,), (0,)), ((), ()))


def product(left, right, contract):
    return lax.dot_general(left, right, contract, preferred_element_type=jnp.float32)


def inside_kernel(base, inside, scale, shift, has_previous, ham, own, inner, current, *rest):
    previous, out = rest if has_previous else (None, rest[0])

    def line(gy, carry):
        above = lax.rem(gy + GY - 1, GY) * GZ
        below = lax.rem(gy + 1, GY) * GZ
        for gz in range(GZ):
            e = gy * GZ + gz
            values = {
                0: own[e],
                inside: inner[e],
                3: own[above + gz],
                4: own[below + gz],
                5: own[gy * GZ + (gz - 1) % GZ],
                6: own[gy * GZ + (gz + 1) % GZ],
            }
            total = None
            for pair in ((0, inside), (3, 4), (5, 6)):
                left = jnp.concatenate([values[d] for d in pair], axis=1)
                right = jnp.concatenate([ham[base + e, d] for d in pair], axis=1)
                term = product(left, right, ROWS)
                total = term if total is None else total + term
            total = scale * total - shift * current[e].astype(jnp.float32)
            if has_previous:
                total = total - previous[e].astype(jnp.float32)
            out[e] = total
        return carry

    lax.fori_loop(0, GY, line, 0)


def outside_kernel(base, direction, scale, ham, halo, partial, rounded, *full):
    def line(gy, carry):
        for gz in range(GZ):
            e = gy * GZ + gz
            value = partial[e] + scale * product(halo[e], ham[base + e, direction], ROWS)
            rounded[e] = value.astype(jnp.bfloat16)
            if full:
                full[0][e] = value
        return carry

    lax.fori_loop(0, GY, line, 0)


def last_kernel(base, direction, scale, ham, halo, partial, other, filtered):
    def line(gy, carry):
        for gz in range(GZ):
            e = gy * GZ + gz
            value = partial[e] + scale * product(halo[e], ham[base + e, direction], ROWS)
            filtered[base + e] = value.astype(jnp.bfloat16)
            filtered[PLANE - base + e] = other[e]
        return carry

    lax.fori_loop(0, GY, line, 0)


def cost(elements, cols, directions):
    size = elements * cols * NB
    read = elements * NB * NB * 2 * directions
    return pl.CostEstimate(flops=2 * size * NB * directions, bytes_accessed=read, transcendentals=0)


def call(kernel, operands, out_shape, estimate, limit, scratch=(), in_specs=None):
    many = isinstance(out_shape, tuple)
    return pl.pallas_call(
        kernel,
        out_shape=out_shape,
        in_specs=in_specs or [VMEM] * len(operands),
        out_specs=(VMEM,) * len(out_shape) if many else VMEM,
        scratch_shapes=scratch,
        cost_estimate=estimate,
        compiler_params=pltpu.CompilerParams(vmem_limit_bytes=limit << 20),
    )(*operands)


def message_kernel(chips, place, mine, other, ritz, ritz_back, ritz_next, ritz_far, out, rows, own):
    held, cols = mine.shape[1], mine.shape[2]

    def fill(parity, source):
        for t in range(chips):
            for el in range(held):
                rows[pl.ds((2 * t + parity) * cols, cols), pl.ds(el * NB, NB)] = source[t, el]

    for t in range(chips):
        for el in range(held):
            own[pl.ds(t * cols, cols), pl.ds(el * NB, NB)] = mine[t, el]

    @pl.when(place[2] == 0)
    def _():
        fill(0, mine)
        fill(1, other)

    @pl.when(place[2] != 0)
    def _():
        fill(1, mine)
        fill(0, other)

    base = chips * cols
    for s in range(0, chips, 2):
        part = product(own[pl.ds(s * cols, 2 * cols), :], rows[...], ROWS).astype(jnp.bfloat16)
        for q in range(2):
            for t in range(chips):
                out[s + q, pl.ds(t * cols, cols), :] = part[q * cols : (q + 1) * cols, t * NB : (t + 1) * NB]
    around = chips // 2
    for away, source in ((0, ritz), (around - 1, ritz_back), (1, ritz_next), (2, ritz_far)):
        turned = product(source[...].reshape(2 * cols, -1), rows[...], PLAIN).astype(jnp.bfloat16)
        for q in range(2):
            to = lax.rem(place[0] + away, around) * 2 + (place[1] if q == 0 else 1 - place[1])
            for el in range(held):
                piece = turned[q * cols : (q + 1) * cols, el * NB : (el + 1) * NB]
                out[to, pl.ds(base + el * cols, cols), :] = piece


def margin_rows_kernel(chips, got, out):
    cols = out.shape[2] // 2
    half = cols // 2
    for t in range(chips):
        total = got[0, pl.ds(t * cols, cols), :].astype(jnp.float32)
        for s in range(1, chips):
            total = total + got[s, pl.ds(t * cols, cols), :].astype(jnp.float32)
        for core in range(2):
            block = total[:, core * cols : (core + 1) * cols]
            out[2 * t + core] = jnp.concatenate([block[:half], block[half:]], axis=1).astype(jnp.bfloat16)


def margin_kernel(scale, got, out):
    total = got[0].astype(jnp.float32)
    for s in range(1, got.shape[0]):
        total = total + got[s].astype(jnp.float32)
    total = total * scale
    half, cols = got.shape[1], out.shape[1]
    out[0:half, :] = total[:, :cols]
    out[half : 2 * half, :] = total[:, cols:]


def whole(hamiltonian, start, ritz):
    slabs = lax.axis_size("z") * lax.axis_size("yh")
    chips = lax.axis_size("x") * lax.axis_size("yl")
    around = lax.axis_size("x")
    rows_total = float(slabs * hamiltonian.shape[0] * NB)
    cols = start.shape[2]
    layer = jax.ShapeDtypeStruct((PLANE, cols, NB), jnp.float32)
    up = [(i, (i + 1) % slabs) for i in range(slabs)]
    down = [((i + 1) % slabs, i) for i in range(slabs)]
    begin = jnp.swapaxes(start, 1, 2)
    base = {"a": 0, "b": PLANE}
    val = {("a", 0): begin[:PLANE], ("b", 0): begin[PLANE:]}
    full = dict(val)
    halo = {}

    def send(name, k):
        if name == "a":
            halo["b", k] = lax.ppermute(val["a", k], ELEM, down)
        else:
            halo["a", k] = lax.ppermute(val["b", k], ELEM, up)

    shared = {}
    source = jnp.swapaxes(ritz, 0, 1)
    across = lax.ppermute(source, "yl", [(0, 1), (1, 0)])
    send("b", 0)
    send("a", 0)
    shared["pair"] = jnp.stack([source, across])
    for shift in (1, around - 1, 2):
        shared[shift] = lax.ppermute(shared["pair"], "x", [(i, (i + shift) % around) for i in range(around)])

    order = []
    for k in range(1, DEG + 1):
        order += [("a", k), ("b", k)] if k % 2 else [("b", k), ("a", k)]
    token = None
    for count, (name, k) in enumerate(order):
        other = "b" if name == "a" else "a"
        inside, outside = (2, 1) if name == "a" else (1, 2)
        own, inner = val[name, k - 1], val[other, k - 1]
        if token is not None:
            own, inner, _ = lax.optimization_barrier((own, inner, token))
        scale = (1.0 if k == 1 else 2.0) / half_width
        operands = [hamiltonian, own, inner, full[name, k - 1]]
        if k > 1:
            operands.append(full[name, k - 2])
        part = call(
            functools.partial(inside_kernel, base[name], inside, scale, scale * center_shift, k > 1),
            operands, layer, cost(PLANE, cols, 6), 12,
        )
        edge = [hamiltonian, halo[name, k - 1], part]
        if count == 2 * DEG - 1:
            filtered = call(
                functools.partial(last_kernel, base[name], outside, scale),
                edge + [val[other, k]],
                jax.ShapeDtypeStruct((2 * PLANE, cols, NB), jnp.bfloat16), cost(PLANE, cols, 1), 12,
            )
            break
        kept = (layer,) if k < DEG else ()
        token, *kept = call(
            functools.partial(outside_kernel, base[name], outside, scale),
            edge, (layer.update(dtype=jnp.bfloat16), *kept), cost(PLANE, cols, 1), 12,
        )
        val[name, k] = token
        if kept:
            full[name, k] = kept[0]
        if k < DEG:
            send(name, k)

    mine = lax.all_to_all(filtered, CHIP, 0, 0, tiled=True)
    mine = mine.reshape(chips, 2 * PLANE // chips, cols, NB)
    theirs = lax.ppermute(mine, "c", [(0, 1), (1, 0)])
    place = jnp.stack([lax.axis_index("x"), lax.axis_index("yl"), lax.axis_index("c")]).astype(jnp.int32)
    held = mine.shape[1]
    depth = held * NB
    sent = call(
        functools.partial(message_kernel, chips),
        (place, mine, theirs, shared["pair"], shared[1], shared[around - 1], shared[2]),
        jax.ShapeDtypeStruct((chips, (chips + held) * cols, NB), jnp.bfloat16),
        pl.CostEstimate(flops=8 * (chips * cols) ** 2 * depth, bytes_accessed=4 << 20, transcendentals=0),
        24,
        (pltpu.VMEM((2 * chips * cols, depth), jnp.bfloat16), pltpu.VMEM((chips * cols, depth), jnp.bfloat16)),
        [SMEM] + [VMEM] * 6,
    )
    got = lax.all_to_all(sent, CHIP, 0, 0, tiled=True)
    small = pl.CostEstimate(flops=1 << 20, bytes_accessed=1 << 20, transcendentals=0)
    rows = call(
        functools.partial(margin_rows_kernel, chips), (got,),
        jax.ShapeDtypeStruct((slabs, cols // 2, 2 * cols), jnp.bfloat16), small, 12,
    )
    rows = lax.all_to_all(rows, ELEM, 0, 0, tiled=True)
    margin = call(
        functools.partial(margin_kernel, 1.0 / rows_total), (rows,),
        jax.ShapeDtypeStruct((cols, cols), jnp.float32), small, 12,
    )
    turned = got[:, chips * cols :].reshape(2 * PLANE, cols, NB).astype(jnp.float32)
    return margin, jnp.swapaxes(turned, 1, 2)


def solution(mesh):
    fine = Mesh(mesh.devices.reshape(8, 2, 4, 2, 2), ("z", "yh", "x", "yl", "c"))
    in_specs = (P(ELEM, None, None, None), P(ELEM, None, ORB), P(None, ORB))
    out_specs = (P(ORB, ELEM), P(ELEM, None, ORB))
    return jax.shard_map(whole, mesh=fine, in_specs=in_specs, out_specs=out_specs, check_vma=False)
```

```python
import functools

import jax
import jax.numpy as jnp
from jax import lax
from jax.experimental import pallas as pl
from jax.experimental.pallas import tpu as pltpu
from jax.sharding import Mesh, PartitionSpec as P


GY = 4
GZ = 4
NB = 128
DEG = 6
PLANE = GY * GZ

center_shift = 0.1
half_width = 1.25

ELEM = ("z", "yh")
ORB = ("x", "yl", "c")
CHIP = ("x", "yl")
VMEM = pl.BlockSpec(memory_space=pltpu.VMEM)
SMEM = pl.BlockSpec(memory_space=pltpu.SMEM)
ROWS = (((1,), (1,)), ((), ()))
PLAIN = (((1,), (0,)), ((), ()))


def product(left, right, contract):
    return lax.dot_general(left, right, contract, preferred_element_type=jnp.float32)


def inside_kernel(base, inside, scale, shift, has_previous, ham, own, inner, current, *rest):
    previous, out = rest if has_previous else (None, rest[0])

    def line(gy, carry):
        above = lax.rem(gy + GY - 1, GY) * GZ
        below = lax.rem(gy + 1, GY) * GZ
        for gz in range(GZ):
            e = gy * GZ + gz
            values = {
                0: own[e],
                inside: inner[e],
                3: own[above + gz],
                4: own[below + gz],
                5: own[gy * GZ + (gz - 1) % GZ],
                6: own[gy * GZ + (gz + 1) % GZ],
            }
            total = None
            for pair in ((0, inside), (3, 4), (5, 6)):
                left = jnp.concatenate([values[d] for d in pair], axis=1)
                right = jnp.concatenate([ham[base + e, d] for d in pair], axis=1)
                term = product(left, right, ROWS)
                total = term if total is None else total + term
            total = scale * total - shift * current[e].astype(jnp.float32)
            if has_previous:
                total = total - previous[e].astype(jnp.float32)
            out[e] = total
        return carry

    lax.fori_loop(0, GY, line, 0)


def outside_kernel(base, direction, scale, ham, halo, partial, rounded, *full):
    def line(gy, carry):
        for gz in range(GZ):
            e = gy * GZ + gz
            value = partial[e] + scale * product(halo[e], ham[base + e, direction], ROWS)
            rounded[e] = value.astype(jnp.bfloat16)
            if full:
                full[0][e] = value
        return carry

    lax.fori_loop(0, GY, line, 0)


def last_kernel(base, direction, scale, ham, halo, partial, other, filtered):
    def line(gy, carry):
        for gz in range(GZ):
            e = gy * GZ + gz
            value = partial[e] + scale * product(halo[e], ham[base + e, direction], ROWS)
            filtered[base + e] = value.astype(jnp.bfloat16)
            filtered[PLANE - base + e] = other[e]
        return carry

    lax.fori_loop(0, GY, line, 0)


def cost(elements, cols, directions):
    size = elements * cols * NB
    read = elements * NB * NB * 2 * directions
    return pl.CostEstimate(flops=2 * size * NB * directions, bytes_accessed=read, transcendentals=0)


def call(kernel, operands, out_shape, estimate, limit, scratch=(), in_specs=None):
    many = isinstance(out_shape, tuple)
    return pl.pallas_call(
        kernel,
        out_shape=out_shape,
        in_specs=in_specs or [VMEM] * len(operands),
        out_specs=(VMEM,) * len(out_shape) if many else VMEM,
        scratch_shapes=scratch,
        cost_estimate=estimate,
        compiler_params=pltpu.CompilerParams(vmem_limit_bytes=limit << 20),
    )(*operands)


def part_kernel(chips, place, mine, other, out, rows, own):
    held, cols = mine.shape[1], mine.shape[2]

    def fill(parity, source):
        for t in range(chips):
            for el in range(held):
                rows[pl.ds((2 * t + parity) * cols, cols), pl.ds(el * NB, NB)] = source[t, el]

    for t in range(chips):
        for el in range(held):
            own[pl.ds(t * cols, cols), pl.ds(el * NB, NB)] = mine[t, el]

    @pl.when(place[2] == 0)
    def _():
        fill(0, mine)
        fill(1, other)

    @pl.when(place[2] != 0)
    def _():
        fill(1, mine)
        fill(0, other)

    for s in range(0, chips, 2):
        part = product(own[pl.ds(s * cols, 2 * cols), :], rows[...], ROWS).astype(jnp.bfloat16)
        for q in range(2):
            for t in range(chips):
                out[s + q, pl.ds(t * cols, cols), :] = part[q * cols : (q + 1) * cols, t * NB : (t + 1) * NB]


def turn_kernel(rows, ritz, ritz_next, ritz_far, ritz_back, *outs):
    held, cols = outs[0].shape[0], outs[0].shape[1]
    for away, source in enumerate((ritz, ritz_next, ritz_far, ritz_back)):
        turned = product(source[...].reshape(2 * cols, -1), rows[...], PLAIN).astype(jnp.bfloat16)
        for q in range(2):
            for el in range(held):
                outs[2 * away + q][el] = turned[q * cols : (q + 1) * cols, el * NB : (el + 1) * NB]


def collect_kernel(around, place, *refs):
    pieces, out = refs[:-1], refs[-1]
    held = pieces[0].shape[0]
    for index, piece in enumerate(pieces):
        away, q = index // 2, index % 2
        line = lax.rem(place[0] + around - away, around) * 2 + (place[1] if q == 0 else 1 - place[1])
        for el in range(held):
            out[line * held + el] = piece[el].astype(jnp.float32)


def margin_rows_kernel(chips, got, out):
    cols = out.shape[2] // 2
    half = cols // 2
    for t in range(chips):
        total = got[0, pl.ds(t * cols, cols), :].astype(jnp.float32)
        for s in range(1, chips):
            total = total + got[s, pl.ds(t * cols, cols), :].astype(jnp.float32)
        for core in range(2):
            block = total[:, core * cols : (core + 1) * cols]
            out[2 * t + core] = jnp.concatenate([block[:half], block[half:]], axis=1).astype(jnp.bfloat16)


def margin_kernel(scale, got, out):
    total = got[0].astype(jnp.float32)
    for s in range(1, got.shape[0]):
        total = total + got[s].astype(jnp.float32)
    total = total * scale
    half, cols = got.shape[1], out.shape[1]
    out[0:half, :] = total[:, :cols]
    out[half : 2 * half, :] = total[:, cols:]


def whole(hamiltonian, start, ritz):
    slabs = lax.axis_size("z") * lax.axis_size("yh")
    chips = lax.axis_size("x") * lax.axis_size("yl")
    around = lax.axis_size("x")
    rows_total = float(slabs * hamiltonian.shape[0] * NB)
    cols = start.shape[2]
    layer = jax.ShapeDtypeStruct((PLANE, cols, NB), jnp.float32)
    up = [(i, (i + 1) % slabs) for i in range(slabs)]
    down = [((i + 1) % slabs, i) for i in range(slabs)]
    begin = jnp.swapaxes(start, 1, 2)
    base = {"a": 0, "b": PLANE}
    val = {("a", 0): begin[:PLANE], ("b", 0): begin[PLANE:]}
    full = dict(val)
    halo = {}

    def send(name, k):
        if name == "a":
            halo["b", k] = lax.ppermute(val["a", k], ELEM, down)
        else:
            halo["a", k] = lax.ppermute(val["b", k], ELEM, up)

    shared = {}
    source = jnp.swapaxes(ritz, 0, 1)
    across = lax.ppermute(source, "yl", [(0, 1), (1, 0)])
    send("b", 0)
    send("a", 0)
    shared["pair"] = jnp.stack([source, across])
    for shift in (1, around - 1, 2):
        shared[shift] = lax.ppermute(shared["pair"], "x", [(i, (i + shift) % around) for i in range(around)])

    order = []
    for k in range(1, DEG + 1):
        order += [("a", k), ("b", k)] if k % 2 else [("b", k), ("a", k)]
    token = None
    for count, (name, k) in enumerate(order):
        other = "b" if name == "a" else "a"
        inside, outside = (2, 1) if name == "a" else (1, 2)
        own, inner = val[name, k - 1], val[other, k - 1]
        if token is not None:
            own, inner, _ = lax.optimization_barrier((own, inner, token))
        scale = (1.0 if k == 1 else 2.0) / half_width
        operands = [hamiltonian, own, inner, full[name, k - 1]]
        if k > 1:
            operands.append(full[name, k - 2])
        part = call(
            functools.partial(inside_kernel, base[name], inside, scale, scale * center_shift, k > 1),
            operands, layer, cost(PLANE, cols, 6), 12,
        )
        edge = [hamiltonian, halo[name, k - 1], part]
        if count == 2 * DEG - 1:
            filtered = call(
                functools.partial(last_kernel, base[name], outside, scale),
                edge + [val[other, k]],
                jax.ShapeDtypeStruct((2 * PLANE, cols, NB), jnp.bfloat16), cost(PLANE, cols, 1), 12,
            )
            break
        kept = (layer,) if k < DEG else ()
        token, *kept = call(
            functools.partial(outside_kernel, base[name], outside, scale),
            edge, (layer.update(dtype=jnp.bfloat16), *kept), cost(PLANE, cols, 1), 12,
        )
        val[name, k] = token
        if kept:
            full[name, k] = kept[0]
        if k < DEG:
            send(name, k)

    mine = lax.all_to_all(filtered, CHIP, 0, 0, tiled=True)
    mine = mine.reshape(chips, 2 * PLANE // chips, cols, NB)
    theirs = lax.ppermute(mine, "c", [(0, 1), (1, 0)])
    place = jnp.stack([lax.axis_index("x"), lax.axis_index("yl"), lax.axis_index("c")]).astype(jnp.int32)
    held = mine.shape[1]
    depth = held * NB
    small = pl.CostEstimate(flops=1 << 20, bytes_accessed=1 << 20, transcendentals=0)
    flops = pl.CostEstimate(flops=4 * (chips * cols) ** 2 * depth, bytes_accessed=2 << 20, transcendentals=0)
    sent, rows = call(
        functools.partial(part_kernel, chips), (place, mine, theirs),
        (
            jax.ShapeDtypeStruct((chips, chips * cols, NB), jnp.bfloat16),
            jax.ShapeDtypeStruct((2 * chips * cols, depth), jnp.bfloat16),
        ),
        flops, 16, (pltpu.VMEM((chips * cols, depth), jnp.bfloat16),), [SMEM, VMEM, VMEM],
    )
    got = lax.all_to_all(sent, CHIP, 0, 0, tiled=True)
    turned = call(
        turn_kernel, (rows, shared["pair"], shared[around - 1], shared[2], shared[1]),
        (jax.ShapeDtypeStruct((held, cols, NB), jnp.bfloat16),) * chips, flops, 16,
    )
    pieces = [turned[0]]
    for index in range(1, chips):
        away, q = index // 2, index % 2
        to = [(i, (i // 2 + away) % around * 2 + (i + q) % 2) for i in range(chips)]
        pieces.append(lax.ppermute(turned[index], CHIP, to))
    total = call(
        functools.partial(margin_rows_kernel, chips), (got,),
        jax.ShapeDtypeStruct((slabs, cols // 2, 2 * cols), jnp.bfloat16), small, 12,
    )
    total = lax.all_to_all(total, ELEM, 0, 0, tiled=True)
    rotated = call(
        functools.partial(collect_kernel, around), (place, *pieces),
        jax.ShapeDtypeStruct((2 * PLANE, cols, NB), jnp.float32), small, 12, (), [SMEM] + [VMEM] * chips,
    )
    margin = call(
        functools.partial(margin_kernel, 1.0 / rows_total), (total,),
        jax.ShapeDtypeStruct((cols, cols), jnp.float32), small, 12,
    )
    return margin, jnp.swapaxes(rotated, 1, 2)


def solution(mesh):
    fine = Mesh(mesh.devices.reshape(8, 2, 4, 2, 2), ("z", "yh", "x", "yl", "c"))
    in_specs = (P(ELEM, None, None, None), P(ELEM, None, ORB), P(None, ORB))
    out_specs = (P(ORB, ELEM), P(ELEM, None, ORB))
    return jax.shard_map(whole, mesh=fine, in_specs=in_specs, out_specs=out_specs, check_vma=False)
```

```python
import functools

import jax
import jax.numpy as jnp
from jax import lax
from jax.experimental import pallas as pl
from jax.experimental.pallas import tpu as pltpu
from jax.sharding import Mesh, PartitionSpec as P


GY = 4
GZ = 4
NB = 128
DEG = 6
PLANE = GY * GZ

center_shift = 0.1
half_width = 1.25

ELEM = ("z", "yh")
ORB = ("x", "yl", "c")
CHIP = ("x", "yl")
VMEM = pl.BlockSpec(memory_space=pltpu.VMEM)
SMEM = pl.BlockSpec(memory_space=pltpu.SMEM)
ROWS = (((1,), (1,)), ((), ()))
PLAIN = (((1,), (0,)), ((), ()))


def product(left, right, contract):
    return lax.dot_general(left, right, contract, preferred_element_type=jnp.float32)


def inside_kernel(base, inside, scale, shift, has_previous, ham, own, inner, current, *rest):
    previous, out = rest if has_previous else (None, rest[0])

    def line(gy, carry):
        above = lax.rem(gy + GY - 1, GY) * GZ
        below = lax.rem(gy + 1, GY) * GZ
        for gz in range(GZ):
            e = gy * GZ + gz
            values = {
                0: own[e],
                inside: inner[e],
                3: own[above + gz],
                4: own[below + gz],
                5: own[gy * GZ + (gz - 1) % GZ],
                6: own[gy * GZ + (gz + 1) % GZ],
            }
            total = None
            for pair in ((0, inside), (3, 4), (5, 6)):
                left = jnp.concatenate([values[d] for d in pair], axis=1)
                right = jnp.concatenate([ham[base + e, d] for d in pair], axis=1)
                term = product(left, right, ROWS)
                total = term if total is None else total + term
            total = scale * total - shift * current[e].astype(jnp.float32)
            if has_previous:
                total = total - previous[e].astype(jnp.float32)
            out[e] = total
        return carry

    lax.fori_loop(0, GY, line, 0)


def outside_kernel(base, direction, scale, ham, halo, partial, rounded, *full):
    def line(gy, carry):
        for gz in range(GZ):
            e = gy * GZ + gz
            value = partial[e] + scale * product(halo[e], ham[base + e, direction], ROWS)
            rounded[e] = value.astype(jnp.bfloat16)
            if full:
                full[0][e] = value
        return carry

    lax.fori_loop(0, GY, line, 0)


def last_kernel(base, direction, scale, ham, halo, partial, other, filtered):
    def line(gy, carry):
        for gz in range(GZ):
            e = gy * GZ + gz
            value = partial[e] + scale * product(halo[e], ham[base + e, direction], ROWS)
            filtered[base + e] = value.astype(jnp.bfloat16)
            filtered[PLANE - base + e] = other[e]
        return carry

    lax.fori_loop(0, GY, line, 0)


def cost(elements, cols, directions):
    size = elements * cols * NB
    read = elements * NB * NB * 2 * directions
    return pl.CostEstimate(flops=2 * size * NB * directions, bytes_accessed=read, transcendentals=0)


def call(kernel, operands, out_shape, estimate, limit, scratch=(), in_specs=None):
    many = isinstance(out_shape, tuple)
    return pl.pallas_call(
        kernel,
        out_shape=out_shape,
        in_specs=in_specs or [VMEM] * len(operands),
        out_specs=(VMEM,) * len(out_shape) if many else VMEM,
        scratch_shapes=scratch,
        cost_estimate=estimate,
        compiler_params=pltpu.CompilerParams(vmem_limit_bytes=limit << 20),
    )(*operands)


def fill_rows(place, mine, other, rows):
    chips, held, cols = mine.shape[0], mine.shape[1], mine.shape[2]

    def fill(parity, source):
        for t in range(chips):
            for el in range(held):
                rows[pl.ds((2 * t + parity) * cols, cols), pl.ds(el * NB, NB)] = source[t, el]

    @pl.when(place[2] == 0)
    def _():
        fill(0, mine)
        fill(1, other)

    @pl.when(place[2] != 0)
    def _():
        fill(1, mine)
        fill(0, other)


def part_blocks(around, away, place, rows, outs):
    chips, cols = outs[0].shape[0], outs[0].shape[1]
    line = lax.rem(place[0] + away, around) * 2
    left = []
    for q in range(2):
        chip = line + (place[1] if q == 0 else 1 - place[1])
        left.append(rows[pl.ds(pl.multiple_of((2 * chip + place[2]) * cols, cols), cols), :])
    part = product(jnp.concatenate(left, axis=0), rows[...], ROWS).astype(jnp.bfloat16)
    for q in range(2):
        for t in range(chips):
            outs[q][t] = part[q * cols : (q + 1) * cols, t * NB : (t + 1) * NB]


def first_part_kernel(around, away, place, mine, other, rows, *outs):
    fill_rows(place, mine, other, rows)
    part_blocks(around, away, place, rows, outs)


def part_kernel(around, away, place, rows, *outs):
    part_blocks(around, away, place, rows, outs)


def turn_kernel(rows, ritz, ritz_next, ritz_far, ritz_back, *outs):
    held, cols = outs[0].shape[0], outs[0].shape[1]
    for away, source in enumerate((ritz, ritz_next, ritz_far, ritz_back)):
        turned = product(source[...].reshape(2 * cols, -1), rows[...], PLAIN).astype(jnp.bfloat16)
        for q in range(2):
            for el in range(held):
                outs[2 * away + q][el] = turned[q * cols : (q + 1) * cols, el * NB : (el + 1) * NB]


def collect_kernel(around, place, *refs):
    pieces, out = refs[:-1], refs[-1]
    held = pieces[0].shape[0]
    for index, piece in enumerate(pieces):
        away, q = index // 2, index % 2
        line = lax.rem(place[0] + around - away, around) * 2 + (place[1] if q == 0 else 1 - place[1])
        for el in range(held):
            out[line * held + el] = piece[el].astype(jnp.float32)


def margin_rows_kernel(*refs):
    pieces, out = refs[:-1], refs[-1]
    cols = out.shape[2] // 2
    half = cols // 2
    for t in range(len(pieces)):
        total = pieces[0][t].astype(jnp.float32)
        for piece in pieces[1:]:
            total = total + piece[t].astype(jnp.float32)
        for core in range(2):
            block = total[:, core * cols : (core + 1) * cols]
            out[2 * t + core] = jnp.concatenate([block[:half], block[half:]], axis=1).astype(jnp.bfloat16)


def margin_kernel(scale, got, out):
    total = got[0].astype(jnp.float32)
    for s in range(1, got.shape[0]):
        total = total + got[s].astype(jnp.float32)
    total = total * scale
    half, cols = got.shape[1], out.shape[1]
    out[0:half, :] = total[:, :cols]
    out[half : 2 * half, :] = total[:, cols:]


def whole(hamiltonian, start, ritz):
    slabs = lax.axis_size("z") * lax.axis_size("yh")
    chips = lax.axis_size("x") * lax.axis_size("yl")
    around = lax.axis_size("x")
    rows_total = float(slabs * hamiltonian.shape[0] * NB)
    cols = start.shape[2]
    layer = jax.ShapeDtypeStruct((PLANE, cols, NB), jnp.float32)
    up = [(i, (i + 1) % slabs) for i in range(slabs)]
    down = [((i + 1) % slabs, i) for i in range(slabs)]
    begin = jnp.swapaxes(start, 1, 2)
    base = {"a": 0, "b": PLANE}
    val = {("a", 0): begin[:PLANE], ("b", 0): begin[PLANE:]}
    full = dict(val)
    halo = {}

    def send(name, k):
        if name == "a":
            halo["b", k] = lax.ppermute(val["a", k], ELEM, down)
        else:
            halo["a", k] = lax.ppermute(val["b", k], ELEM, up)

    shared = {}
    source = jnp.swapaxes(ritz, 0, 1)
    across = lax.ppermute(source, "yl", [(0, 1), (1, 0)])
    send("b", 0)
    send("a", 0)
    shared["pair"] = jnp.stack([source, across])
    for shift in (1, around - 1, 2):
        shared[shift] = lax.ppermute(shared["pair"], "x", [(i, (i + shift) % around) for i in range(around)])

    order = []
    for k in range(1, DEG + 1):
        order += [("a", k), ("b", k)] if k % 2 else [("b", k), ("a", k)]
    token = None
    for count, (name, k) in enumerate(order):
        other = "b" if name == "a" else "a"
        inside, outside = (2, 1) if name == "a" else (1, 2)
        own, inner = val[name, k - 1], val[other, k - 1]
        if token is not None:
            own, inner, _ = lax.optimization_barrier((own, inner, token))
        scale = (1.0 if k == 1 else 2.0) / half_width
        operands = [hamiltonian, own, inner, full[name, k - 1]]
        if k > 1:
            operands.append(full[name, k - 2])
        part = call(
            functools.partial(inside_kernel, base[name], inside, scale, scale * center_shift, k > 1),
            operands, layer, cost(PLANE, cols, 6), 12,
        )
        edge = [hamiltonian, halo[name, k - 1], part]
        if count == 2 * DEG - 1:
            filtered = call(
                functools.partial(last_kernel, base[name], outside, scale),
                edge + [val[other, k]],
                jax.ShapeDtypeStruct((2 * PLANE, cols, NB), jnp.bfloat16), cost(PLANE, cols, 1), 12,
            )
            break
        kept = (layer,) if k < DEG else ()
        token, *kept = call(
            functools.partial(outside_kernel, base[name], outside, scale),
            edge, (layer.update(dtype=jnp.bfloat16), *kept), cost(PLANE, cols, 1), 12,
        )
        val[name, k] = token
        if kept:
            full[name, k] = kept[0]
        if k < DEG:
            send(name, k)

    mine = lax.all_to_all(filtered, CHIP, 0, 0, tiled=True)
    mine = mine.reshape(chips, 2 * PLANE // chips, cols, NB)
    theirs = lax.ppermute(mine, "c", [(0, 1), (1, 0)])
    place = jnp.stack([lax.axis_index("x"), lax.axis_index("yl"), lax.axis_index("c")]).astype(jnp.int32)
    held = mine.shape[1]
    depth = held * NB
    small = pl.CostEstimate(flops=1 << 20, bytes_accessed=1 << 20, transcendentals=0)
    flops = pl.CostEstimate(flops=4 * (chips * cols) ** 2 * depth, bytes_accessed=2 << 20, transcendentals=0)

    def to_chip(away, q):
        return [(i, (i // 2 + away) % around * 2 + (i + q) % 2) for i in range(chips)]

    block = jax.ShapeDtypeStruct((chips, cols, NB), jnp.bfloat16)
    rows = None
    parts = []
    for away in (1, around - 1, 2, 0):
        if rows is None:
            rows, *blocks = call(
                functools.partial(first_part_kernel, around, away), (place, mine, theirs),
                (jax.ShapeDtypeStruct((2 * chips * cols, depth), jnp.bfloat16), block, block),
                flops, 16, (), [SMEM, VMEM, VMEM],
            )
        else:
            blocks = call(
                functools.partial(part_kernel, around, away), (place, rows),
                (block, block), flops, 16, (), [SMEM, VMEM],
            )
        for q in range(2):
            if away == 0 and q == 0:
                parts.append(blocks[0])
                continue
            parts.append(lax.ppermute(blocks[q], CHIP, to_chip(away, q)))
    turned = call(
        turn_kernel, (rows, shared["pair"], shared[around - 1], shared[2], shared[1]),
        (jax.ShapeDtypeStruct((held, cols, NB), jnp.bfloat16),) * chips, flops, 16,
    )
    pieces = [turned[0]]
    for index in range(1, chips):
        pieces.append(lax.ppermute(turned[index], CHIP, to_chip(index // 2, index % 2)))
    total = call(
        margin_rows_kernel, parts,
        jax.ShapeDtypeStruct((slabs, cols // 2, 2 * cols), jnp.bfloat16), small, 12,
    )
    total = lax.all_to_all(total, ELEM, 0, 0, tiled=True)
    rotated = call(
        functools.partial(collect_kernel, around), (place, *pieces),
        jax.ShapeDtypeStruct((2 * PLANE, cols, NB), jnp.float32), small, 12, (), [SMEM] + [VMEM] * chips,
    )
    margin = call(
        functools.partial(margin_kernel, 1.0 / rows_total), (total,),
        jax.ShapeDtypeStruct((cols, cols), jnp.float32), small, 12,
    )
    return margin, jnp.swapaxes(rotated, 1, 2)


def solution(mesh):
    fine = Mesh(mesh.devices.reshape(8, 2, 4, 2, 2), ("z", "yh", "x", "yl", "c"))
    in_specs = (P(ELEM, None, None, None), P(ELEM, None, ORB), P(None, ORB))
    out_specs = (P(ORB, ELEM), P(ELEM, None, ORB))
    return jax.shard_map(whole, mesh=fine, in_specs=in_specs, out_specs=out_specs, check_vma=False)
```

```python
import functools

import jax
import jax.numpy as jnp
from jax import lax
from jax.experimental import pallas as pl
from jax.experimental.pallas import tpu as pltpu
from jax.sharding import Mesh, PartitionSpec as P


GY = 4
GZ = 4
NB = 128
DEG = 6
PLANE = GY * GZ

center_shift = 0.1
half_width = 1.25

ELEM = ("z", "yh")
ORB = ("x", "yl", "c")
CHIP = ("x", "yl")
VMEM = pl.BlockSpec(memory_space=pltpu.VMEM)
SMEM = pl.BlockSpec(memory_space=pltpu.SMEM)
ROWS = (((1,), (1,)), ((), ()))
PLAIN = (((1,), (0,)), ((), ()))


def product(left, right, contract):
    return lax.dot_general(left, right, contract, preferred_element_type=jnp.float32)


def inside_kernel(base, inside, scale, shift, has_previous, ham, own, inner, current, *rest):
    previous, out = rest if has_previous else (None, rest[0])

    def line(gy, carry):
        above = lax.rem(gy + GY - 1, GY) * GZ
        below = lax.rem(gy + 1, GY) * GZ
        for gz in range(GZ):
            e = gy * GZ + gz
            values = {
                0: own[e],
                inside: inner[e],
                3: own[above + gz],
                4: own[below + gz],
                5: own[gy * GZ + (gz - 1) % GZ],
                6: own[gy * GZ + (gz + 1) % GZ],
            }
            total = None
            for pair in ((0, inside), (3, 4), (5, 6)):
                left = jnp.concatenate([values[d] for d in pair], axis=1)
                right = jnp.concatenate([ham[base + e, d] for d in pair], axis=1)
                term = product(left, right, ROWS)
                total = term if total is None else total + term
            total = scale * total - shift * current[e].astype(jnp.float32)
            if has_previous:
                total = total - previous[e].astype(jnp.float32)
            out[e] = total
        return carry

    lax.fori_loop(0, GY, line, 0)


def outside_kernel(base, direction, scale, ham, halo, partial, rounded, *full):
    def line(gy, carry):
        for gz in range(GZ):
            e = gy * GZ + gz
            value = partial[e] + scale * product(halo[e], ham[base + e, direction], ROWS)
            rounded[e] = value.astype(jnp.bfloat16)
            if full:
                full[0][e] = value
        return carry

    lax.fori_loop(0, GY, line, 0)


def last_kernel(base, direction, scale, ham, halo, partial, other, filtered):
    def line(gy, carry):
        for gz in range(GZ):
            e = gy * GZ + gz
            value = partial[e] + scale * product(halo[e], ham[base + e, direction], ROWS)
            filtered[base + e] = value.astype(jnp.bfloat16)
            filtered[PLANE - base + e] = other[e]
        return carry

    lax.fori_loop(0, GY, line, 0)


def cost(elements, cols, directions):
    size = elements * cols * NB
    read = elements * NB * NB * 2 * directions
    return pl.CostEstimate(flops=2 * size * NB * directions, bytes_accessed=read, transcendentals=0)


def call(kernel, operands, out_shape, estimate, limit, scratch=(), in_specs=None):
    many = isinstance(out_shape, tuple)
    return pl.pallas_call(
        kernel,
        out_shape=out_shape,
        in_specs=in_specs or [VMEM] * len(operands),
        out_specs=(VMEM,) * len(out_shape) if many else VMEM,
        scratch_shapes=scratch,
        cost_estimate=estimate,
        compiler_params=pltpu.CompilerParams(vmem_limit_bytes=limit << 20),
    )(*operands)


def fill_rows(place, mine, other, rows):
    chips, held, cols = mine.shape[0], mine.shape[1], mine.shape[2]

    def fill(parity, source):
        for t in range(chips):
            for el in range(held):
                rows[pl.ds((2 * t + parity) * cols, cols), pl.ds(el * NB, NB)] = source[t, el]

    @pl.when(place[2] == 0)
    def _():
        fill(0, mine)
        fill(1, other)

    @pl.when(place[2] != 0)
    def _():
        fill(1, mine)
        fill(0, other)


def part_blocks(around, away, place, rows, outs):
    chips, cols = outs[0].shape[0], outs[0].shape[1]
    line = lax.rem(place[0] + away, around) * 2
    left = []
    for q in range(2):
        chip = line + (place[1] if q == 0 else 1 - place[1])
        left.append(rows[pl.ds(pl.multiple_of((2 * chip + place[2]) * cols, cols), cols), :])
    part = product(jnp.concatenate(left, axis=0), rows[...], ROWS).astype(jnp.bfloat16)
    for q in range(2):
        for t in range(chips):
            outs[q][t] = part[q * cols : (q + 1) * cols, t * NB : (t + 1) * NB]


def first_part_kernel(around, away, place, mine, other, rows, *outs):
    fill_rows(place, mine, other, rows)
    part_blocks(around, away, place, rows, outs)


def part_kernel(around, away, place, rows, *outs):
    part_blocks(around, away, place, rows, outs)


def turn_kernel(rows, ritz, ritz_next, ritz_far, ritz_back, *outs):
    held, cols = outs[0].shape[0], outs[0].shape[1]
    for away, source in enumerate((ritz, ritz_next, ritz_far, ritz_back)):
        turned = product(source[...].reshape(2 * cols, -1), rows[...], PLAIN).astype(jnp.bfloat16)
        for el in range(held):
            outs[away][el] = turned[:cols, el * NB : (el + 1) * NB]
            outs[4][away, el] = turned[cols:, el * NB : (el + 1) * NB]


def join_kernel(crossed, *refs):
    count = len(refs) // 2
    for away in range(count):
        refs[count + away][0] = refs[away][...]
        refs[count + away][1] = crossed[away + 1]


def collect_kernel(around, place, here, crossed, *refs):
    pieces, out = refs[:-1], refs[-1]
    held = here.shape[0]
    for q in range(2):
        near = place[1] if q == 0 else 1 - place[1]
        for away in range(around):
            line = lax.rem(place[0] + around - away, around) * 2 + near
            for el in range(held):
                if away:
                    piece = pieces[away - 1][q, el]
                else:
                    piece = crossed[0, el] if q else here[el]
                out[line * held + el] = piece.astype(jnp.float32)


def margin_rows_kernel(*refs):
    pieces, out = refs[:-1], refs[-1]
    cols = out.shape[2] // 2
    half = cols // 2
    for t in range(len(pieces)):
        total = pieces[0][t].astype(jnp.float32)
        for piece in pieces[1:]:
            total = total + piece[t].astype(jnp.float32)
        for core in range(2):
            block = total[:, core * cols : (core + 1) * cols]
            out[2 * t + core] = jnp.concatenate([block[:half], block[half:]], axis=1).astype(jnp.bfloat16)


def margin_kernel(scale, got, out):
    total = got[0].astype(jnp.float32)
    for s in range(1, got.shape[0]):
        total = total + got[s].astype(jnp.float32)
    total = total * scale
    half, cols = got.shape[1], out.shape[1]
    out[0:half, :] = total[:, :cols]
    out[half : 2 * half, :] = total[:, cols:]


def whole(hamiltonian, start, ritz):
    slabs = lax.axis_size("z") * lax.axis_size("yh")
    chips = lax.axis_size("x") * lax.axis_size("yl")
    around = lax.axis_size("x")
    rows_total = float(slabs * hamiltonian.shape[0] * NB)
    cols = start.shape[2]
    layer = jax.ShapeDtypeStruct((PLANE, cols, NB), jnp.float32)
    up = [(i, (i + 1) % slabs) for i in range(slabs)]
    down = [((i + 1) % slabs, i) for i in range(slabs)]
    begin = jnp.swapaxes(start, 1, 2)
    base = {"a": 0, "b": PLANE}
    val = {("a", 0): begin[:PLANE], ("b", 0): begin[PLANE:]}
    full = dict(val)
    halo = {}

    def send(name, k):
        if name == "a":
            halo["b", k] = lax.ppermute(val["a", k], ELEM, down)
        else:
            halo["a", k] = lax.ppermute(val["b", k], ELEM, up)

    shared = {}
    source = jnp.swapaxes(ritz, 0, 1)
    across = lax.ppermute(source, "yl", [(0, 1), (1, 0)])
    send("b", 0)
    send("a", 0)
    shared["pair"] = jnp.stack([source, across])
    for shift in (1, around - 1, 2):
        shared[shift] = lax.ppermute(shared["pair"], "x", [(i, (i + shift) % around) for i in range(around)])

    order = []
    for k in range(1, DEG + 1):
        order += [("a", k), ("b", k)] if k % 2 else [("b", k), ("a", k)]
    token = None
    for count, (name, k) in enumerate(order):
        other = "b" if name == "a" else "a"
        inside, outside = (2, 1) if name == "a" else (1, 2)
        own, inner = val[name, k - 1], val[other, k - 1]
        if token is not None:
            own, inner, _ = lax.optimization_barrier((own, inner, token))
        scale = (1.0 if k == 1 else 2.0) / half_width
        operands = [hamiltonian, own, inner, full[name, k - 1]]
        if k > 1:
            operands.append(full[name, k - 2])
        part = call(
            functools.partial(inside_kernel, base[name], inside, scale, scale * center_shift, k > 1),
            operands, layer, cost(PLANE, cols, 6), 12,
        )
        edge = [hamiltonian, halo[name, k - 1], part]
        if count == 2 * DEG - 1:
            filtered = call(
                functools.partial(last_kernel, base[name], outside, scale),
                edge + [val[other, k]],
                jax.ShapeDtypeStruct((2 * PLANE, cols, NB), jnp.bfloat16), cost(PLANE, cols, 1), 12,
            )
            break
        kept = (layer,) if k < DEG else ()
        token, *kept = call(
            functools.partial(outside_kernel, base[name], outside, scale),
            edge, (layer.update(dtype=jnp.bfloat16), *kept), cost(PLANE, cols, 1), 12,
        )
        val[name, k] = token
        if kept:
            full[name, k] = kept[0]
        if k < DEG:
            send(name, k)

    mine = lax.all_to_all(filtered, CHIP, 0, 0, tiled=True)
    mine = mine.reshape(chips, 2 * PLANE // chips, cols, NB)
    theirs = lax.ppermute(mine, "c", [(0, 1), (1, 0)])
    place = jnp.stack([lax.axis_index("x"), lax.axis_index("yl"), lax.axis_index("c")]).astype(jnp.int32)
    held = mine.shape[1]
    depth = held * NB
    small = pl.CostEstimate(flops=1 << 20, bytes_accessed=1 << 20, transcendentals=0)
    flops = pl.CostEstimate(flops=4 * (chips * cols) ** 2 * depth, bytes_accessed=2 << 20, transcendentals=0)

    def to_chip(away, q):
        return [(i, (i // 2 + away) % around * 2 + (i + q) % 2) for i in range(chips)]

    block = jax.ShapeDtypeStruct((chips, cols, NB), jnp.bfloat16)
    rows = None
    parts = []
    for away in (2, 1, around - 1, 0):
        if rows is None:
            rows, *blocks = call(
                functools.partial(first_part_kernel, around, away), (place, mine, theirs),
                (jax.ShapeDtypeStruct((2 * chips * cols, depth), jnp.bfloat16), block, block),
                flops, 16, (), [SMEM, VMEM, VMEM],
            )
        else:
            blocks = call(
                functools.partial(part_kernel, around, away), (place, rows),
                (block, block), flops, 16, (), [SMEM, VMEM],
            )
        for q in range(2):
            if away == 0 and q == 0:
                parts.append(blocks[0])
                continue
            parts.append(lax.ppermute(blocks[q], CHIP, to_chip(away, q)))
    piece = jax.ShapeDtypeStruct((held, cols, NB), jnp.bfloat16)
    *turned, across = call(
        turn_kernel, (rows, shared["pair"], shared[around - 1], shared[2], shared[1]),
        (piece,) * around + (piece.update(shape=(around, *piece.shape)),), flops, 16,
    )
    crossed = lax.ppermute(across, "yl", [(0, 1), (1, 0)])
    total = call(
        margin_rows_kernel, parts,
        jax.ShapeDtypeStruct((slabs, cols // 2, 2 * cols), jnp.bfloat16), small, 12,
    )
    total = lax.all_to_all(total, ELEM, 0, 0, tiled=True)
    joined = call(
        join_kernel, (crossed, *turned[1:]),
        (piece.update(shape=(2, *piece.shape)),) * (around - 1), small, 12,
    )
    pieces = []
    for away in range(1, around):
        pieces.append(lax.ppermute(joined[away - 1], "x", [(i, (i + away) % around) for i in range(around)]))
    rotated = call(
        functools.partial(collect_kernel, around), (place, turned[0], crossed, *pieces),
        jax.ShapeDtypeStruct((2 * PLANE, cols, NB), jnp.float32), small, 12, (), [SMEM] + [VMEM] * (around + 1),
    )
    margin = call(
        functools.partial(margin_kernel, 1.0 / rows_total), (total,),
        jax.ShapeDtypeStruct((cols, cols), jnp.float32), small, 12,
    )
    return margin, jnp.swapaxes(rotated, 1, 2)


def solution(mesh):
    fine = Mesh(mesh.devices.reshape(8, 2, 4, 2, 2), ("z", "yh", "x", "yl", "c"))
    in_specs = (P(ELEM, None, None, None), P(ELEM, None, ORB), P(None, ORB))
    out_specs = (P(ORB, ELEM), P(ELEM, None, ORB))
    return jax.shard_map(whole, mesh=fine, in_specs=in_specs, out_specs=out_specs, check_vma=False)
```

```python
import functools

import jax
import jax.numpy as jnp
from jax import lax
from jax.experimental import pallas as pl
from jax.experimental.pallas import tpu as pltpu
from jax.sharding import Mesh, PartitionSpec as P


GY = 4
GZ = 4
NB = 128
DEG = 6
PLANE = GY * GZ

center_shift = 0.1
half_width = 1.25

ELEM = ("z", "yh")
ORB = ("x", "yl", "c")
CHIP = ("x", "yl")
VMEM = pl.BlockSpec(memory_space=pltpu.VMEM)
SMEM = pl.BlockSpec(memory_space=pltpu.SMEM)
ROWS = (((1,), (1,)), ((), ()))
PLAIN = (((1,), (0,)), ((), ()))


def product(left, right, contract):
    return lax.dot_general(left, right, contract, preferred_element_type=jnp.float32)


def inside_kernel(base, inside, scale, shift, has_previous, ham, own, inner, current, *rest):
    previous, out = rest if has_previous else (None, rest[0])

    def line(gy, carry):
        above = lax.rem(gy + GY - 1, GY) * GZ
        below = lax.rem(gy + 1, GY) * GZ
        for gz in range(GZ):
            e = gy * GZ + gz
            values = {
                0: own[e],
                inside: inner[e],
                3: own[above + gz],
                4: own[below + gz],
                5: own[gy * GZ + (gz - 1) % GZ],
                6: own[gy * GZ + (gz + 1) % GZ],
            }
            total = None
            for pair in ((0, inside), (3, 4), (5, 6)):
                left = jnp.concatenate([values[d] for d in pair], axis=1)
                right = jnp.concatenate([ham[base + e, d] for d in pair], axis=1)
                term = product(left, right, ROWS)
                total = term if total is None else total + term
            total = scale * total - shift * current[e].astype(jnp.float32)
            if has_previous:
                total = total - previous[e].astype(jnp.float32)
            out[e] = total
        return carry

    lax.fori_loop(0, GY, line, 0)


def outside_kernel(base, direction, scale, ham, halo, partial, rounded, *full):
    def line(gy, carry):
        for gz in range(GZ):
            e = gy * GZ + gz
            value = partial[e] + scale * product(halo[e], ham[base + e, direction], ROWS)
            rounded[e] = value.astype(jnp.bfloat16)
            if full:
                full[0][e] = value
        return carry

    lax.fori_loop(0, GY, line, 0)


def last_kernel(base, direction, scale, ham, halo, partial, other, filtered):
    def line(gy, carry):
        for gz in range(GZ):
            e = gy * GZ + gz
            value = partial[e] + scale * product(halo[e], ham[base + e, direction], ROWS)
            filtered[base + e] = value.astype(jnp.bfloat16)
            filtered[PLANE - base + e] = other[e]
        return carry

    lax.fori_loop(0, GY, line, 0)


def cost(elements, cols, directions):
    size = elements * cols * NB
    read = elements * NB * NB * 2 * directions
    return pl.CostEstimate(flops=2 * size * NB * directions, bytes_accessed=read, transcendentals=0)


def call(kernel, operands, out_shape, estimate, limit, scratch=(), in_specs=None):
    many = isinstance(out_shape, tuple)
    return pl.pallas_call(
        kernel,
        out_shape=out_shape,
        in_specs=in_specs or [VMEM] * len(operands),
        out_specs=(VMEM,) * len(out_shape) if many else VMEM,
        scratch_shapes=scratch,
        cost_estimate=estimate,
        compiler_params=pltpu.CompilerParams(vmem_limit_bytes=limit << 20),
    )(*operands)


def fill_rows(place, mine, other, rows):
    chips, held, cols = mine.shape[0], mine.shape[1], mine.shape[2]

    def fill(parity, source):
        for t in range(chips):
            for el in range(held):
                rows[pl.ds((2 * t + parity) * cols, cols), pl.ds(el * NB, NB)] = source[t, el]

    @pl.when(place[3] == 0)
    def _():
        fill(0, mine)
        fill(1, other)

    @pl.when(place[3] != 0)
    def _():
        fill(1, mine)
        fill(0, other)


def part_blocks(around, away, place, rows, outs):
    chips, cols = outs[0].shape[0], outs[0].shape[1]
    line = lax.rem(place[0] + away, around) * 2
    left = []
    for q in range(2):
        chip = line + (place[1] if q == 0 else 1 - place[1])
        left.append(rows[pl.ds(pl.multiple_of((2 * chip + place[2]) * cols, cols), cols), :])
    part = product(jnp.concatenate(left, axis=0), rows[...], ROWS).astype(jnp.bfloat16)
    for q in range(2):
        for t in range(chips):
            outs[q][t] = part[q * cols : (q + 1) * cols, t * NB : (t + 1) * NB]


def first_part_kernel(around, away, place, mine, other, rows, *outs):
    fill_rows(place, mine, other, rows)
    part_blocks(around, away, place, rows, outs)


def part_kernel(around, away, place, rows, *outs):
    part_blocks(around, away, place, rows, outs)


def turn_kernel(rows, ritz, ritz_next, ritz_far, ritz_back, *outs):
    held, cols = outs[0].shape[0], outs[0].shape[1]
    for away, source in enumerate((ritz, ritz_next, ritz_far, ritz_back)):
        turned = product(source[...].reshape(2 * cols, -1), rows[...], PLAIN).astype(jnp.bfloat16)
        for el in range(held):
            outs[away][el] = turned[:cols, el * NB : (el + 1) * NB]
            outs[4][away, el] = turned[cols:, el * NB : (el + 1) * NB]


def join_kernel(crossed, *refs):
    count = len(refs) // 2
    for away in range(count):
        refs[count + away][0] = refs[away][...]
        refs[count + away][1] = crossed[away + 1]


def collect_kernel(around, place, here, crossed, *refs):
    pieces, out = refs[:-1], refs[-1]
    held = here.shape[0]
    for q in range(2):
        near = place[1] if q == 0 else 1 - place[1]
        for away in range(around):
            line = lax.rem(place[0] + around - away, around) * 2 + near
            for el in range(held):
                if away:
                    piece = pieces[away - 1][q, el]
                else:
                    piece = crossed[0, el] if q else here[el]
                out[line * held + el] = piece.astype(jnp.float32)


def margin_rows_kernel(*refs):
    pieces, out = refs[:-1], refs[-1]
    cols = out.shape[2] // 2
    half = cols // 2
    for t in range(len(pieces)):
        total = pieces[0][t].astype(jnp.float32)
        for piece in pieces[1:]:
            total = total + piece[t].astype(jnp.float32)
        for core in range(2):
            block = total[:, core * cols : (core + 1) * cols]
            out[2 * t + core] = jnp.concatenate([block[:half], block[half:]], axis=1).astype(jnp.bfloat16)


def margin_kernel(scale, got, out):
    total = got[0].astype(jnp.float32)
    for s in range(1, got.shape[0]):
        total = total + got[s].astype(jnp.float32)
    total = total * scale
    half, cols = got.shape[1], out.shape[1]
    out[0:half, :] = total[:, :cols]
    out[half : 2 * half, :] = total[:, cols:]


def whole(hamiltonian, start, ritz):
    slabs = lax.axis_size("z") * lax.axis_size("yh")
    chips = lax.axis_size("x") * lax.axis_size("yl")
    around = lax.axis_size("x")
    rows_total = float(slabs * hamiltonian.shape[0] * NB)
    cols = start.shape[2]
    layer = jax.ShapeDtypeStruct((PLANE, cols, NB), jnp.float32)
    up = [(2 * i + c, 2 * ((i + 1) % slabs) + 1 - c) for i in range(slabs) for c in range(2)]
    down = [(to, source) for source, to in up]
    base = {"a": 0, "b": PLANE}
    halo = {}

    def send(name, k):
        if name == "a":
            halo["b", k] = lax.ppermute(val["a", k], ELEM + ("c",), down)
        else:
            halo["a", k] = lax.ppermute(val["b", k], ELEM + ("c",), up)

    shared = {}
    source = jnp.swapaxes(ritz, 0, 1)
    across = lax.ppermute(source, "yl", [(0, 1), (1, 0)])
    begin = lax.ppermute(jnp.swapaxes(start, 1, 2), ("yh", "c"), [(0, 0), (1, 1), (2, 3), (3, 2)])
    val = {("a", 0): begin[:PLANE], ("b", 0): begin[PLANE:]}
    full = dict(val)
    send("b", 0)
    send("a", 0)
    shared["pair"] = jnp.stack([source, across])
    for shift in (1, around - 1, 2):
        shared[shift] = lax.ppermute(shared["pair"], "x", [(i, (i + shift) % around) for i in range(around)])

    order = []
    for k in range(1, DEG + 1):
        order += [("a", k), ("b", k)] if k % 2 else [("b", k), ("a", k)]
    token = None
    for count, (name, k) in enumerate(order):
        other = "b" if name == "a" else "a"
        inside, outside = (2, 1) if name == "a" else (1, 2)
        own, inner = val[name, k - 1], val[other, k - 1]
        if token is not None:
            own, inner, _ = lax.optimization_barrier((own, inner, token))
        scale = (1.0 if k == 1 else 2.0) / half_width
        operands = [hamiltonian, own, inner, full[name, k - 1]]
        if k > 1:
            operands.append(full[name, k - 2])
        part = call(
            functools.partial(inside_kernel, base[name], inside, scale, scale * center_shift, k > 1),
            operands, layer, cost(PLANE, cols, 6), 12,
        )
        edge = [hamiltonian, halo[name, k - 1], part]
        if count == 2 * DEG - 1:
            filtered = call(
                functools.partial(last_kernel, base[name], outside, scale),
                edge + [val[other, k]],
                jax.ShapeDtypeStruct((2 * PLANE, cols, NB), jnp.bfloat16), cost(PLANE, cols, 1), 12,
            )
            break
        kept = (layer,) if k < DEG else ()
        token, *kept = call(
            functools.partial(outside_kernel, base[name], outside, scale),
            edge, (layer.update(dtype=jnp.bfloat16), *kept), cost(PLANE, cols, 1), 12,
        )
        val[name, k] = token
        if kept:
            full[name, k] = kept[0]
        if k < DEG:
            send(name, k)

    mine = lax.all_to_all(filtered, CHIP, 0, 0, tiled=True)
    mine = mine.reshape(chips, 2 * PLANE // chips, cols, NB)
    theirs = lax.ppermute(mine, "c", [(0, 1), (1, 0)])
    core = lax.axis_index("c")
    place = jnp.stack([lax.axis_index("x"), lax.axis_index("yl"), core, (core + lax.axis_index("yh")) % 2]).astype(jnp.int32)
    held = mine.shape[1]
    depth = held * NB
    small = pl.CostEstimate(flops=1 << 20, bytes_accessed=1 << 20, transcendentals=0)
    flops = pl.CostEstimate(flops=4 * (chips * cols) ** 2 * depth, bytes_accessed=2 << 20, transcendentals=0)

    def to_chip(away, q):
        return [(i, (i // 2 + away) % around * 2 + (i + q) % 2) for i in range(chips)]

    block = jax.ShapeDtypeStruct((chips, cols, NB), jnp.bfloat16)
    rows = None
    parts = []
    for away in (0, 2, 1, around - 1):
        if rows is None:
            rows, *blocks = call(
                functools.partial(first_part_kernel, around, away), (place, mine, theirs),
                (jax.ShapeDtypeStruct((2 * chips * cols, depth), jnp.bfloat16), block, block),
                flops, 16, (), [SMEM, VMEM, VMEM],
            )
        else:
            blocks = call(
                functools.partial(part_kernel, around, away), (place, rows),
                (block, block), flops, 16, (), [SMEM, VMEM],
            )
        for q in (1, 0):
            if away == 0 and q == 0:
                parts.append(blocks[0])
                continue
            parts.append(lax.ppermute(blocks[q], CHIP, to_chip(away, q)))
    piece = jax.ShapeDtypeStruct((held, cols, NB), jnp.bfloat16)
    *turned, across = call(
        turn_kernel, (rows, shared["pair"], shared[around - 1], shared[2], shared[1]),
        (piece,) * around + (piece.update(shape=(around, *piece.shape)),), flops, 16,
    )
    crossed = lax.ppermute(across, "yl", [(0, 1), (1, 0)])
    total = call(
        margin_rows_kernel, parts,
        jax.ShapeDtypeStruct((slabs, cols // 2, 2 * cols), jnp.bfloat16), small, 12,
    )
    total = lax.all_to_all(total, ELEM, 0, 0, tiled=True)
    joined = call(
        join_kernel, (crossed, *turned[1:]),
        (piece.update(shape=(2, *piece.shape)),) * (around - 1), small, 12,
    )
    pieces = []
    for away in range(1, around):
        pieces.append(lax.ppermute(joined[away - 1], "x", [(i, (i + away) % around) for i in range(around)]))
    rotated = call(
        functools.partial(collect_kernel, around), (place, turned[0], crossed, *pieces),
        jax.ShapeDtypeStruct((2 * PLANE, cols, NB), jnp.float32), small, 12, (), [SMEM] + [VMEM] * (around + 1),
    )
    margin = call(
        functools.partial(margin_kernel, 1.0 / rows_total), (total,),
        jax.ShapeDtypeStruct((cols, cols), jnp.float32), small, 12,
    )
    return margin, jnp.swapaxes(rotated, 1, 2)


def solution(mesh):
    fine = Mesh(mesh.devices.reshape(8, 2, 4, 2, 2), ("z", "yh", "x", "yl", "c"))
    in_specs = (P(ELEM, None, None, None), P(ELEM, None, ORB), P(None, ORB))
    out_specs = (P(ORB, ELEM), P(ELEM, None, ORB))
    return jax.shard_map(whole, mesh=fine, in_specs=in_specs, out_specs=out_specs, check_vma=False)
```

```python
import functools

import jax
import jax.numpy as jnp
from jax import lax
from jax.experimental import pallas as pl
from jax.experimental.pallas import tpu as pltpu
from jax.sharding import Mesh, PartitionSpec as P


GY = 4
GZ = 4
NB = 128
DEG = 6
PLANE = GY * GZ

center_shift = 0.1
half_width = 1.25

ELEM = ("z", "yh")
ORB = ("x", "yl", "c")
CHIP = ("x", "yl")
VMEM = pl.BlockSpec(memory_space=pltpu.VMEM)
SMEM = pl.BlockSpec(memory_space=pltpu.SMEM)
ROWS = (((1,), (1,)), ((), ()))
PLAIN = (((1,), (0,)), ((), ()))


def product(left, right, contract):
    return lax.dot_general(left, right, contract, preferred_element_type=jnp.float32)


def inside_kernel(base, inside, scale, shift, has_previous, ham, own, inner, current, *rest):
    previous, out = rest if has_previous else (None, rest[0])

    def line(gy, carry):
        above = lax.rem(gy + GY - 1, GY) * GZ
        below = lax.rem(gy + 1, GY) * GZ
        for gz in range(GZ):
            e = gy * GZ + gz
            values = {
                0: own[e],
                inside: inner[e],
                3: own[above + gz],
                4: own[below + gz],
                5: own[gy * GZ + (gz - 1) % GZ],
                6: own[gy * GZ + (gz + 1) % GZ],
            }
            total = None
            for pair in ((0, inside), (3, 4), (5, 6)):
                left = jnp.concatenate([values[d] for d in pair], axis=1)
                right = jnp.concatenate([ham[base + e, d] for d in pair], axis=1)
                term = product(left, right, ROWS)
                total = term if total is None else total + term
            total = scale * total - shift * current[e].astype(jnp.float32)
            if has_previous:
                total = total - previous[e].astype(jnp.float32)
            out[e] = total
        return carry

    lax.fori_loop(0, GY, line, 0)


def outside_kernel(base, direction, scale, ham, halo, partial, rounded, *full):
    def line(gy, carry):
        for gz in range(GZ):
            e = gy * GZ + gz
            value = partial[e] + scale * product(halo[e], ham[base + e, direction], ROWS)
            rounded[e] = value.astype(jnp.bfloat16)
            if full:
                full[0][e] = value
        return carry

    lax.fori_loop(0, GY, line, 0)


def last_kernel(base, direction, scale, ham, halo, partial, other, filtered):
    def line(gy, carry):
        for gz in range(GZ):
            e = gy * GZ + gz
            value = partial[e] + scale * product(halo[e], ham[base + e, direction], ROWS)
            filtered[base + e] = value.astype(jnp.bfloat16)
            filtered[PLANE - base + e] = other[e]
        return carry

    lax.fori_loop(0, GY, line, 0)


def cost(elements, cols, directions):
    size = elements * cols * NB
    read = elements * NB * NB * 2 * directions
    return pl.CostEstimate(flops=2 * size * NB * directions, bytes_accessed=read, transcendentals=0)


def call(kernel, operands, out_shape, estimate, limit, scratch=(), in_specs=None):
    many = isinstance(out_shape, tuple)
    return pl.pallas_call(
        kernel,
        out_shape=out_shape,
        in_specs=in_specs or [VMEM] * len(operands),
        out_specs=(VMEM,) * len(out_shape) if many else VMEM,
        scratch_shapes=scratch,
        cost_estimate=estimate,
        compiler_params=pltpu.CompilerParams(vmem_limit_bytes=limit << 20),
    )(*operands)


def fill_rows(place, mine, other, rows):
    chips, held, cols = mine.shape[0], mine.shape[1], mine.shape[2]

    def fill(parity, source):
        for t in range(chips):
            for el in range(held):
                rows[pl.ds((2 * t + parity) * cols, cols), pl.ds(el * NB, NB)] = source[t, el]

    @pl.when(place[2] == 0)
    def _():
        fill(0, mine)
        fill(1, other)

    @pl.when(place[2] != 0)
    def _():
        fill(1, mine)
        fill(0, other)


def part_blocks(around, away, place, rows, outs):
    chips, cols = outs[0].shape[0], outs[0].shape[1]
    line = lax.rem(place[0] + away, around) * 2
    left = []
    for q in range(2):
        chip = line + (place[1] if q == 0 else 1 - place[1])
        left.append(rows[pl.ds(pl.multiple_of((2 * chip + place[2]) * cols, cols), cols), :])
    part = product(jnp.concatenate(left, axis=0), rows[...], ROWS).astype(jnp.bfloat16)
    for q in range(2):
        for t in range(chips):
            outs[q][t] = part[q * cols : (q + 1) * cols, t * NB : (t + 1) * NB]


def first_part_kernel(around, away, place, mine, other, rows, *outs):
    fill_rows(place, mine, other, rows)
    part_blocks(around, away, place, rows, outs)


def part_kernel(around, away, place, rows, *outs):
    part_blocks(around, away, place, rows, outs)


def turn_kernel(rows, ritz, ritz_next, ritz_far, ritz_back, *outs):
    held, cols = outs[0].shape[0], outs[0].shape[1]
    for away, source in enumerate((ritz, ritz_next, ritz_far, ritz_back)):
        turned = product(source[...].reshape(2 * cols, -1), rows[...], PLAIN).astype(jnp.bfloat16)
        for el in range(held):
            outs[away][el] = turned[:cols, el * NB : (el + 1) * NB]
            outs[4][away, el] = turned[cols:, el * NB : (el + 1) * NB]


def part_ways_kernel(crossed, *outs):
    for away, out in enumerate(outs):
        out[...] = crossed[away + 1]


def collect_kernel(around, place, here, crossed, *refs):
    pieces, out = refs[:-1], refs[-1]
    held = here.shape[0]
    for q in range(2):
        near = place[1] if q == 0 else 1 - place[1]
        for away in range(around):
            line = lax.rem(place[0] + around - away, around) * 2 + near
            for el in range(held):
                if away:
                    piece = pieces[q * (around - 1) + away - 1][el]
                else:
                    piece = crossed[0, el] if q else here[el]
                out[line * held + el] = piece.astype(jnp.float32)


def margin_rows_kernel(*refs):
    pieces, out = refs[:-1], refs[-1]
    cols = out.shape[2] // 2
    half = cols // 2
    for t in range(len(pieces)):
        total = pieces[0][t].astype(jnp.float32)
        for piece in pieces[1:]:
            total = total + piece[t].astype(jnp.float32)
        for core in range(2):
            block = total[:, core * cols : (core + 1) * cols]
            out[2 * t + core] = jnp.concatenate([block[:half], block[half:]], axis=1).astype(jnp.bfloat16)


def margin_kernel(scale, got, out):
    total = got[0].astype(jnp.float32)
    for s in range(1, got.shape[0]):
        total = total + got[s].astype(jnp.float32)
    total = total * scale
    half, cols = got.shape[1], out.shape[1]
    out[0:half, :] = total[:, :cols]
    out[half : 2 * half, :] = total[:, cols:]


def whole(hamiltonian, start, ritz):
    slabs = lax.axis_size("z") * lax.axis_size("yh")
    chips = lax.axis_size("x") * lax.axis_size("yl")
    around = lax.axis_size("x")
    rows_total = float(slabs * hamiltonian.shape[0] * NB)
    cols = start.shape[2]
    layer = jax.ShapeDtypeStruct((PLANE, cols, NB), jnp.float32)
    up = [(i, (i + 1) % slabs) for i in range(slabs)]
    down = [((i + 1) % slabs, i) for i in range(slabs)]
    begin = jnp.swapaxes(start, 1, 2)
    val = {("a", 0): begin[:PLANE], ("b", 0): begin[PLANE:]}
    full = dict(val)
    base = {"a": 0, "b": PLANE}
    halo = {}

    def send(name, k):
        if name == "a":
            halo["b", k] = lax.ppermute(val["a", k], ELEM, down)
        else:
            halo["a", k] = lax.ppermute(val["b", k], ELEM, up)

    shared = {}
    source = jnp.swapaxes(ritz, 0, 1)
    across = lax.ppermute(source, "yl", [(0, 1), (1, 0)])
    send("b", 0)
    send("a", 0)
    shared["pair"] = jnp.stack([source, across])
    for shift in (1, around - 1, 2):
        shared[shift] = lax.ppermute(shared["pair"], "x", [(i, (i + shift) % around) for i in range(around)])

    order = []
    for k in range(1, DEG + 1):
        order += [("a", k), ("b", k)] if k % 2 else [("b", k), ("a", k)]
    token = None
    for count, (name, k) in enumerate(order):
        other = "b" if name == "a" else "a"
        inside, outside = (2, 1) if name == "a" else (1, 2)
        own, inner = val[name, k - 1], val[other, k - 1]
        if token is not None:
            own, inner, _ = lax.optimization_barrier((own, inner, token))
        scale = (1.0 if k == 1 else 2.0) / half_width
        operands = [hamiltonian, own, inner, full[name, k - 1]]
        if k > 1:
            operands.append(full[name, k - 2])
        part = call(
            functools.partial(inside_kernel, base[name], inside, scale, scale * center_shift, k > 1),
            operands, layer, cost(PLANE, cols, 6), 12,
        )
        edge = [hamiltonian, halo[name, k - 1], part]
        if count == 2 * DEG - 1:
            filtered = call(
                functools.partial(last_kernel, base[name], outside, scale),
                edge + [val[other, k]],
                jax.ShapeDtypeStruct((2 * PLANE, cols, NB), jnp.bfloat16), cost(PLANE, cols, 1), 12,
            )
            break
        kept = (layer,) if k < DEG else ()
        token, *kept = call(
            functools.partial(outside_kernel, base[name], outside, scale),
            edge, (layer.update(dtype=jnp.bfloat16), *kept), cost(PLANE, cols, 1), 12,
        )
        val[name, k] = token
        if kept:
            full[name, k] = kept[0]
        if k < DEG:
            send(name, k)

    mine = lax.all_to_all(filtered, CHIP, 0, 0, tiled=True)
    mine = mine.reshape(chips, 2 * PLANE // chips, cols, NB)
    theirs = lax.ppermute(mine, "c", [(0, 1), (1, 0)])
    place = jnp.stack([lax.axis_index("x"), lax.axis_index("yl"), lax.axis_index("c")]).astype(jnp.int32)
    held = mine.shape[1]
    depth = held * NB
    small = pl.CostEstimate(flops=1 << 20, bytes_accessed=1 << 20, transcendentals=0)
    flops = pl.CostEstimate(flops=4 * (chips * cols) ** 2 * depth, bytes_accessed=2 << 20, transcendentals=0)

    def to_chip(away, q):
        return [(i, (i // 2 + away) % around * 2 + (i + q) % 2) for i in range(chips)]

    block = jax.ShapeDtypeStruct((chips, cols, NB), jnp.bfloat16)
    rows = None
    parts = []
    for away in (0, 2, 1, around - 1):
        if rows is None:
            rows, *blocks = call(
                functools.partial(first_part_kernel, around, away), (place, mine, theirs),
                (jax.ShapeDtypeStruct((2 * chips * cols, depth), jnp.bfloat16), block, block),
                flops, 16, (), [SMEM, VMEM, VMEM],
            )
        else:
            blocks = call(
                functools.partial(part_kernel, around, away), (place, rows),
                (block, block), flops, 16, (), [SMEM, VMEM],
            )
        for q in (1, 0):
            if away == 0 and q == 0:
                parts.append(blocks[0])
                continue
            parts.append(lax.ppermute(blocks[q], CHIP, to_chip(away, q)))
    piece = jax.ShapeDtypeStruct((held, cols, NB), jnp.bfloat16)
    *turned, across = call(
        turn_kernel, (rows, shared["pair"], shared[around - 1], shared[2], shared[1]),
        (piece,) * around + (piece.update(shape=(around, *piece.shape)),), flops, 16,
    )
    crossed = lax.ppermute(across, "yl", [(0, 1), (1, 0)])
    pieces = []

    def along(away, value):
        pieces.append(lax.ppermute(value, "x", [(i, (i + away) % around) for i in range(around)]))

    for away in range(1, around):
        along(away, turned[away])
    total = call(
        margin_rows_kernel, parts,
        jax.ShapeDtypeStruct((slabs, cols // 2, 2 * cols), jnp.bfloat16), small, 12,
    )
    total = lax.all_to_all(total, ELEM, 0, 0, tiled=True)
    ways = call(part_ways_kernel, (crossed,), (piece,) * (around - 1), small, 12)
    for away in range(1, around):
        along(away, ways[away - 1])
    rotated = call(
        functools.partial(collect_kernel, around), (place, turned[0], crossed, *pieces),
        jax.ShapeDtypeStruct((2 * PLANE, cols, NB), jnp.float32), small, 12, (), [SMEM] + [VMEM] * (2 * around),
    )
    margin = call(
        functools.partial(margin_kernel, 1.0 / rows_total), (total,),
        jax.ShapeDtypeStruct((cols, cols), jnp.float32), small, 12,
    )
    return margin, jnp.swapaxes(rotated, 1, 2)


def solution(mesh):
    fine = Mesh(mesh.devices.reshape(8, 2, 4, 2, 2), ("z", "yh", "x", "yl", "c"))
    in_specs = (P(ELEM, None, None, None), P(ELEM, None, ORB), P(None, ORB))
    out_specs = (P(ORB, ELEM), P(ELEM, None, ORB))
    return jax.shard_map(whole, mesh=fine, in_specs=in_specs, out_specs=out_specs, check_vma=False)
```

```python
import functools

import jax
import jax.numpy as jnp
from jax import lax
from jax.experimental import pallas as pl
from jax.experimental.pallas import tpu as pltpu
from jax.sharding import Mesh, PartitionSpec as P


GY = 4
GZ = 4
NB = 128
DEG = 6
PLANE = GY * GZ

center_shift = 0.1
half_width = 1.25

ELEM = ("z", "yh")
ORB = ("x", "yl", "c")
CHIP = ("x", "yl")
VMEM = pl.BlockSpec(memory_space=pltpu.VMEM)
SMEM = pl.BlockSpec(memory_space=pltpu.SMEM)
PLAIN = (((1,), (0,)), ((), ()))


def product(left, right, contract):
    return lax.dot_general(left, right, contract, preferred_element_type=jnp.float32)


def inside_kernel(base, inside, scale, shift, has_previous, ham, own, inner, current, *rest):
    previous, out = rest if has_previous else (None, rest[0])

    def line(gy, carry):
        above = lax.rem(gy + GY - 1, GY) * GZ
        below = lax.rem(gy + 1, GY) * GZ
        for gz in range(GZ):
            e = gy * GZ + gz
            left_z, right_z = gy * GZ + (gz - 1) % GZ, gy * GZ + (gz + 1) % GZ
            terms = (
                (own[e], ham[base + e, 0], inner[e], ham[PLANE - base + e, 3 - inside]),
                (own[above + gz], ham[base + above + gz, 4], own[below + gz], ham[base + below + gz, 3]),
                (own[left_z], ham[base + left_z, 6], own[right_z], ham[base + right_z, 5]),
            )
            total = None
            for v0, h0, v1, h1 in terms:
                left, right = jnp.concatenate([v0, v1], axis=1), jnp.concatenate([h0, h1], axis=0)
                term = product(left, right, PLAIN)
                total = term if total is None else total + term
            total = scale * total - shift * current[e].astype(jnp.float32)
            if has_previous:
                total = total - previous[e].astype(jnp.float32)
            out[e] = total
        return carry

    lax.fori_loop(0, GY, line, 0)


def edges_kernel(ham, edge_a, edge_b):
    def line(gy, carry):
        for gz in range(GZ):
            e = gy * GZ + gz
            edge_a[e] = ham[e, 1].T
            edge_b[e] = ham[PLANE + e, 2].T
        return carry

    lax.fori_loop(0, GY, line, 0)


def outside_kernel(scale, edge, halo, partial, rounded, *full):
    def line(gy, carry):
        for gz in range(GZ):
            e = gy * GZ + gz
            value = partial[e] + scale * product(halo[e], edge[e], PLAIN)
            rounded[e] = value.astype(jnp.bfloat16)
            if full:
                full[0][e] = value
        return carry

    lax.fori_loop(0, GY, line, 0)


def last_kernel(base, scale, edge, halo, partial, other, filtered):
    def line(gy, carry):
        for gz in range(GZ):
            e = gy * GZ + gz
            value = partial[e] + scale * product(halo[e], edge[e], PLAIN)
            filtered[base + e] = value.astype(jnp.bfloat16)
            filtered[PLANE - base + e] = other[e]
        return carry

    lax.fori_loop(0, GY, line, 0)


def cost(elements, cols, directions):
    size = elements * cols * NB
    read = elements * NB * NB * 2 * directions
    return pl.CostEstimate(flops=2 * size * NB * directions, bytes_accessed=read, transcendentals=0)


def call(kernel, operands, out_shape, estimate, limit, scratch=(), in_specs=None):
    many = isinstance(out_shape, tuple)
    return pl.pallas_call(
        kernel,
        out_shape=out_shape,
        in_specs=in_specs or [VMEM] * len(operands),
        out_specs=(VMEM,) * len(out_shape) if many else VMEM,
        scratch_shapes=scratch,
        cost_estimate=estimate,
        compiler_params=pltpu.CompilerParams(vmem_limit_bytes=limit << 20),
    )(*operands)


def turn_kernel(place, mine, other, ritz, ritz_next, ritz_far, ritz_back, rows, *outs):
    chips, held, cols = mine.shape[0], mine.shape[1], mine.shape[2]

    def fill(parity, source):
        for t in range(chips):
            for el in range(held):
                rows[pl.ds((2 * t + parity) * cols, cols), pl.ds(el * NB, NB)] = source[t, el]

    @pl.when(place[2] == 0)
    def _():
        fill(0, mine)
        fill(1, other)

    @pl.when(place[2] != 0)
    def _():
        fill(1, mine)
        fill(0, other)

    for away, source in enumerate((ritz, ritz_next, ritz_far, ritz_back)):
        turned = product(source[...].reshape(2 * cols, -1), rows[...], PLAIN).astype(jnp.bfloat16)
        for el in range(held):
            outs[away][el] = turned[:cols, el * NB : (el + 1) * NB]
            outs[4][away, el] = turned[cols:, el * NB : (el + 1) * NB]


def part_blocks(around, away, place, rows, across, outs):
    chips, cols = outs[0].shape[0], outs[0].shape[1]
    line = lax.rem(place[0] + away, around) * 2
    left = []
    for q in range(2):
        chip = line + (place[1] if q == 0 else 1 - place[1])
        left.append(rows[pl.ds(pl.multiple_of((2 * chip + place[2]) * cols, cols), cols), :])
    part = product(jnp.concatenate(left, axis=0), across[...], PLAIN).astype(jnp.bfloat16)
    for q in range(2):
        for t in range(chips):
            outs[q][t] = part[q * cols : (q + 1) * cols, t * NB : (t + 1) * NB]


def first_part_kernel(around, away, place, rows, across, *outs):
    for t in range(rows.shape[0] // NB):
        for el in range(rows.shape[1] // NB):
            across[pl.ds(el * NB, NB), pl.ds(t * NB, NB)] = rows[pl.ds(t * NB, NB), pl.ds(el * NB, NB)].T
    part_blocks(around, away, place, rows, across, outs)


def part_kernel(around, away, place, rows, across, *outs):
    part_blocks(around, away, place, rows, across, outs)


def join_kernel(crossed, *refs):
    count = len(refs) // 2
    for away in range(count):
        refs[count + away][0] = refs[away][...]
        refs[count + away][1] = crossed[away + 1]


def collect_kernel(around, place, here, crossed, *refs):
    pieces, out = refs[:-1], refs[-1]
    held = here.shape[0]
    for q in range(2):
        near = place[1] if q == 0 else 1 - place[1]
        for away in range(around):
            line = lax.rem(place[0] + around - away, around) * 2 + near
            for el in range(held):
                if away:
                    piece = pieces[away - 1][q, el]
                else:
                    piece = crossed[0, el] if q else here[el]
                out[line * held + el] = piece.astype(jnp.float32)


def margin_rows_kernel(*refs):
    pieces, out = refs[:-1], refs[-1]
    cols = out.shape[2] // 2
    half = cols // 2
    for t in range(len(pieces)):
        total = pieces[0][t].astype(jnp.float32)
        for piece in pieces[1:]:
            total = total + piece[t].astype(jnp.float32)
        for core in range(2):
            block = total[:, core * cols : (core + 1) * cols]
            out[2 * t + core] = jnp.concatenate([block[:half], block[half:]], axis=1).astype(jnp.bfloat16)


def margin_kernel(scale, got, out):
    total = got[0].astype(jnp.float32)
    for s in range(1, got.shape[0]):
        total = total + got[s].astype(jnp.float32)
    total = total * scale
    half, cols = got.shape[1], out.shape[1]
    out[0:half, :] = total[:, :cols]
    out[half : 2 * half, :] = total[:, cols:]


def whole(hamiltonian, start, ritz):
    slabs = lax.axis_size("z") * lax.axis_size("yh")
    chips = lax.axis_size("x") * lax.axis_size("yl")
    around = lax.axis_size("x")
    rows_total = float(slabs * hamiltonian.shape[0] * NB)
    cols = start.shape[2]
    layer = jax.ShapeDtypeStruct((PLANE, cols, NB), jnp.float32)
    up = [(i, (i + 1) % slabs) for i in range(slabs)]
    down = [((i + 1) % slabs, i) for i in range(slabs)]
    begin = jnp.swapaxes(start, 1, 2)
    val = {("a", 0): begin[:PLANE], ("b", 0): begin[PLANE:]}
    full = dict(val)
    base = {"a": 0, "b": PLANE}
    halo = {}

    def send(name, k):
        if name == "a":
            halo["b", k] = lax.ppermute(val["a", k], ELEM, down)
        else:
            halo["a", k] = lax.ppermute(val["b", k], ELEM, up)

    shared = {}
    source = jnp.swapaxes(ritz, 0, 1)
    across = lax.ppermute(source, "yl", [(0, 1), (1, 0)])
    send("b", 0)
    send("a", 0)
    shared["pair"] = jnp.stack([source, across])
    for shift in (1, around - 1, 2):
        shared[shift] = lax.ppermute(shared["pair"], "x", [(i, (i + shift) % around) for i in range(around)])

    order = []
    for k in range(1, DEG + 1):
        order += [("a", k), ("b", k)] if k % 2 else [("b", k), ("a", k)]
    token = None
    blocks = jax.ShapeDtypeStruct((PLANE, NB, NB), jnp.bfloat16)
    edges = call(edges_kernel, (hamiltonian,), (blocks, blocks), cost(PLANE, cols, 2), 12)
    edges = dict(zip("ab", edges))
    for count, (name, k) in enumerate(order):
        other = "b" if name == "a" else "a"
        inside = 2 if name == "a" else 1
        own, inner = val[name, k - 1], val[other, k - 1]
        if token is not None:
            own, inner, _ = lax.optimization_barrier((own, inner, token))
        scale = (1.0 if k == 1 else 2.0) / half_width
        operands = [hamiltonian, own, inner, full[name, k - 1]]
        if k > 1:
            operands.append(full[name, k - 2])
        part = call(
            functools.partial(inside_kernel, base[name], inside, scale, scale * center_shift, k > 1),
            operands, layer, cost(PLANE, cols, 6), 12,
        )
        edge = [edges[name], halo[name, k - 1], part]
        if count == 2 * DEG - 1:
            filtered = call(
                functools.partial(last_kernel, base[name], scale),
                edge + [val[other, k]],
                jax.ShapeDtypeStruct((2 * PLANE, cols, NB), jnp.bfloat16), cost(PLANE, cols, 1), 12,
            )
            break
        kept = (layer,) if k < DEG else ()
        token, *kept = call(
            functools.partial(outside_kernel, scale),
            edge, (layer.update(dtype=jnp.bfloat16), *kept), cost(PLANE, cols, 1), 12,
        )
        val[name, k] = token
        if kept:
            full[name, k] = kept[0]
        if k < DEG:
            send(name, k)

    mine = lax.all_to_all(filtered, CHIP, 0, 0, tiled=True)
    mine = mine.reshape(chips, 2 * PLANE // chips, cols, NB)
    theirs = lax.ppermute(mine, "c", [(0, 1), (1, 0)])
    place = jnp.stack([lax.axis_index("x"), lax.axis_index("yl"), lax.axis_index("c")]).astype(jnp.int32)
    held = mine.shape[1]
    depth = held * NB
    small = pl.CostEstimate(flops=1 << 20, bytes_accessed=1 << 20, transcendentals=0)
    flops = pl.CostEstimate(flops=4 * (chips * cols) ** 2 * depth, bytes_accessed=2 << 20, transcendentals=0)

    def to_chip(away, q):
        return [(i, (i // 2 + away) % around * 2 + (i + q) % 2) for i in range(chips)]

    piece = jax.ShapeDtypeStruct((held, cols, NB), jnp.bfloat16)
    rows, *turned, other_y = call(
        turn_kernel,
        (place, mine, theirs, shared["pair"], shared[around - 1], shared[2], shared[1]),
        (
            jax.ShapeDtypeStruct((2 * chips * cols, depth), jnp.bfloat16),
            *(piece,) * around,
            piece.update(shape=(around, *piece.shape)),
        ),
        flops, 16, (), [SMEM] + [VMEM] * 6,
    )
    crossed = lax.ppermute(other_y, "yl", [(0, 1), (1, 0)])

    block = jax.ShapeDtypeStruct((chips, cols, NB), jnp.bfloat16)
    across = None
    parts = []
    for away in (0, 2, 1, around - 1):
        if across is None:
            across, *blocks = call(
                functools.partial(first_part_kernel, around, away), (place, rows),
                (jax.ShapeDtypeStruct((depth, 2 * chips * cols), jnp.bfloat16), block, block),
                flops, 16, (), [SMEM, VMEM],
            )
        else:
            blocks = call(
                functools.partial(part_kernel, around, away), (place, rows, across),
                (block, block), flops, 16, (), [SMEM, VMEM, VMEM],
            )
        for q in (1, 0):
            if away == 0 and q == 0:
                parts.append(blocks[0])
                continue
            parts.append(lax.ppermute(blocks[q], CHIP, to_chip(away, q)))
    joined = call(
        join_kernel, (crossed, *turned[1:]),
        (piece.update(shape=(2, *piece.shape)),) * (around - 1), small, 12,
    )
    pieces = []
    for away in range(1, around):
        pieces.append(lax.ppermute(joined[away - 1], "x", [(i, (i + away) % around) for i in range(around)]))
    total = call(
        margin_rows_kernel, parts,
        jax.ShapeDtypeStruct((slabs, cols // 2, 2 * cols), jnp.bfloat16), small, 12,
    )
    total = lax.all_to_all(total, ELEM, 0, 0, tiled=True)
    rotated = call(
        functools.partial(collect_kernel, around), (place, turned[0], crossed, *pieces),
        jax.ShapeDtypeStruct((2 * PLANE, cols, NB), jnp.float32), small, 12, (), [SMEM] + [VMEM] * (around + 1),
    )
    margin = call(
        functools.partial(margin_kernel, 1.0 / rows_total), (total,),
        jax.ShapeDtypeStruct((cols, cols), jnp.float32), small, 12,
    )
    return margin, jnp.swapaxes(rotated, 1, 2)


def solution(mesh):
    fine = Mesh(mesh.devices.reshape(8, 2, 4, 2, 2), ("z", "yh", "x", "yl", "c"))
    in_specs = (P(ELEM, None, None, None), P(ELEM, None, ORB), P(None, ORB))
    out_specs = (P(ORB, ELEM), P(ELEM, None, ORB))
    return jax.shard_map(whole, mesh=fine, in_specs=in_specs, out_specs=out_specs, check_vma=False)
```

```python
import functools

import jax
import jax.numpy as jnp
from jax import lax
from jax.experimental import pallas as pl
from jax.experimental.pallas import tpu as pltpu
from jax.sharding import Mesh, PartitionSpec as P


GY = 4
GZ = 4
NB = 128
DEG = 6
PLANE = GY * GZ

center_shift = 0.1
half_width = 1.25

ELEM = ("z", "yh")
ORB = ("x", "yl", "c")
CHIP = ("x", "yl")
VMEM = pl.BlockSpec(memory_space=pltpu.VMEM)
SMEM = pl.BlockSpec(memory_space=pltpu.SMEM)
PLAIN = (((1,), (0,)), ((), ()))


def product(left, right, contract):
    return lax.dot_general(left, right, contract, preferred_element_type=jnp.float32)


def inside_kernel(base, inside, scale, shift, has_previous, ham, own, inner, current, *rest):
    previous, out = rest if has_previous else (None, rest[0])

    def line(gy, carry):
        above = lax.rem(gy + GY - 1, GY) * GZ
        below = lax.rem(gy + 1, GY) * GZ
        for gz in range(GZ):
            e = gy * GZ + gz
            left_z, right_z = gy * GZ + (gz - 1) % GZ, gy * GZ + (gz + 1) % GZ
            terms = (
                (own[e], ham[base + e, 0], inner[e], ham[PLANE - base + e, 3 - inside]),
                (own[above + gz], ham[base + above + gz, 4], own[below + gz], ham[base + below + gz, 3]),
                (own[left_z], ham[base + left_z, 6], own[right_z], ham[base + right_z, 5]),
            )
            total = None
            for v0, h0, v1, h1 in terms:
                left, right = jnp.concatenate([v0, v1], axis=1), jnp.concatenate([h0, h1], axis=0)
                term = product(left, right, PLAIN)
                total = term if total is None else total + term
            total = scale * total - shift * current[e].astype(jnp.float32)
            if has_previous:
                total = total - previous[e].astype(jnp.float32)
            out[e] = total
        return carry

    lax.fori_loop(0, GY, line, 0)


def edges_kernel(ham, edge_a, edge_b):
    def line(gy, carry):
        for gz in range(GZ):
            e = gy * GZ + gz
            edge_a[e] = ham[e, 1].T
            edge_b[e] = ham[PLANE + e, 2].T
        return carry

    lax.fori_loop(0, GY, line, 0)


def outside_kernel(scale, edge, halo, partial, rounded, *full):
    def line(gy, carry):
        for gz in range(GZ):
            e = gy * GZ + gz
            value = partial[e] + scale * product(halo[e], edge[e], PLAIN)
            rounded[e] = value.astype(jnp.bfloat16)
            if full:
                full[0][e] = value
        return carry

    lax.fori_loop(0, GY, line, 0)


def last_kernel(base, scale, edge, halo, partial, other, filtered):
    def line(gy, carry):
        for gz in range(GZ):
            e = gy * GZ + gz
            value = partial[e] + scale * product(halo[e], edge[e], PLAIN)
            filtered[base + e] = value.astype(jnp.bfloat16)
            filtered[PLANE - base + e] = other[e]
        return carry

    lax.fori_loop(0, GY, line, 0)


def cost(elements, cols, directions):
    size = elements * cols * NB
    read = elements * NB * NB * 2 * directions
    return pl.CostEstimate(flops=2 * size * NB * directions, bytes_accessed=read, transcendentals=0)


def call(kernel, operands, out_shape, estimate, limit, scratch=(), in_specs=None):
    many = isinstance(out_shape, tuple)
    return pl.pallas_call(
        kernel,
        out_shape=out_shape,
        in_specs=in_specs or [VMEM] * len(operands),
        out_specs=(VMEM,) * len(out_shape) if many else VMEM,
        scratch_shapes=scratch,
        cost_estimate=estimate,
        compiler_params=pltpu.CompilerParams(vmem_limit_bytes=limit << 20),
    )(*operands)


def part_kernel(around, place, mine, other, rows, *refs):
    outs, across = refs[:-1], refs[-1]
    chips, held, cols = mine.shape[0], mine.shape[1], mine.shape[2]

    def fill(parity, source):
        for t in range(chips):
            for el in range(held):
                rows[pl.ds((2 * t + parity) * cols, cols), pl.ds(el * NB, NB)] = source[t, el]

    @pl.when(place[2] == 0)
    def _():
        fill(0, mine)
        fill(1, other)

    @pl.when(place[2] != 0)
    def _():
        fill(1, mine)
        fill(0, other)

    for t in range(chips):
        for el in range(held):
            across[pl.ds(el * NB, NB), pl.ds(t * NB, NB)] = rows[pl.ds(t * NB, NB), pl.ds(el * NB, NB)].T
    for away in range(around):
        line = lax.rem(place[0] + away, around) * 2
        left = []
        for q in range(2):
            chip = line + (place[1] if q == 0 else 1 - place[1])
            left.append(rows[pl.ds(pl.multiple_of((2 * chip + place[2]) * cols, cols), cols), :])
        part = product(jnp.concatenate(left, axis=0), across[...], PLAIN).astype(jnp.bfloat16)
        for q in range(2):
            for t in range(chips):
                outs[2 * away + q][t] = part[q * cols : (q + 1) * cols, t * NB : (t + 1) * NB]


def turn_kernel(rows, ritz, ritz_next, ritz_far, ritz_back, *outs):
    held, cols = outs[0].shape[0], outs[0].shape[1]
    for away, source in enumerate((ritz, ritz_next, ritz_far, ritz_back)):
        turned = product(source[...].reshape(2 * cols, -1), rows[...], PLAIN).astype(jnp.bfloat16)
        for el in range(held):
            outs[away][el] = turned[:cols, el * NB : (el + 1) * NB]
            outs[4][away, el] = turned[cols:, el * NB : (el + 1) * NB]


def part_ways_kernel(crossed, *outs):
    for away, out in enumerate(outs):
        out[...] = crossed[away + 1]


def collect_kernel(around, place, here, crossed, *refs):
    pieces, out = refs[:-1], refs[-1]
    held = here.shape[0]
    for q in range(2):
        near = place[1] if q == 0 else 1 - place[1]
        for away in range(around):
            line = lax.rem(place[0] + around - away, around) * 2 + near
            for el in range(held):
                if away:
                    piece = pieces[q * (around - 1) + away - 1][el]
                else:
                    piece = crossed[0, el] if q else here[el]
                out[line * held + el] = piece.astype(jnp.float32)


def margin_rows_kernel(*refs):
    pieces, out = refs[:-1], refs[-1]
    cols = out.shape[2] // 2
    half = cols // 2
    for t in range(len(pieces)):
        total = pieces[0][t].astype(jnp.float32)
        for piece in pieces[1:]:
            total = total + piece[t].astype(jnp.float32)
        for core in range(2):
            block = total[:, core * cols : (core + 1) * cols]
            out[2 * t + core] = jnp.concatenate([block[:half], block[half:]], axis=1).astype(jnp.bfloat16)


def margin_kernel(scale, got, out):
    total = got[0].astype(jnp.float32)
    for s in range(1, got.shape[0]):
        total = total + got[s].astype(jnp.float32)
    total = total * scale
    half, cols = got.shape[1], out.shape[1]
    out[0:half, :] = total[:, :cols]
    out[half : 2 * half, :] = total[:, cols:]


def whole(hamiltonian, start, ritz):
    slabs = lax.axis_size("z") * lax.axis_size("yh")
    chips = lax.axis_size("x") * lax.axis_size("yl")
    around = lax.axis_size("x")
    rows_total = float(slabs * hamiltonian.shape[0] * NB)
    cols = start.shape[2]
    layer = jax.ShapeDtypeStruct((PLANE, cols, NB), jnp.float32)
    up = [(i, (i + 1) % slabs) for i in range(slabs)]
    down = [((i + 1) % slabs, i) for i in range(slabs)]
    begin = jnp.swapaxes(start, 1, 2)
    val = {("a", 0): begin[:PLANE], ("b", 0): begin[PLANE:]}
    full = dict(val)
    base = {"a": 0, "b": PLANE}
    halo = {}

    def send(name, k):
        if name == "a":
            halo["b", k] = lax.ppermute(val["a", k], ELEM, down)
        else:
            halo["a", k] = lax.ppermute(val["b", k], ELEM, up)

    shared = {}
    source = jnp.swapaxes(ritz, 0, 1)
    across = lax.ppermute(source, "yl", [(0, 1), (1, 0)])
    send("b", 0)
    send("a", 0)
    shared["pair"] = jnp.stack([source, across])
    for shift in (1, around - 1, 2):
        shared[shift] = lax.ppermute(shared["pair"], "x", [(i, (i + shift) % around) for i in range(around)])

    order = []
    for k in range(1, DEG + 1):
        order += [("a", k), ("b", k)] if k % 2 else [("b", k), ("a", k)]
    token = None
    blocks = jax.ShapeDtypeStruct((PLANE, NB, NB), jnp.bfloat16)
    edges = call(edges_kernel, (hamiltonian,), (blocks, blocks), cost(PLANE, cols, 2), 12)
    edges = dict(zip("ab", edges))
    for count, (name, k) in enumerate(order):
        other = "b" if name == "a" else "a"
        inside = 2 if name == "a" else 1
        own, inner = val[name, k - 1], val[other, k - 1]
        if token is not None:
            own, inner, _ = lax.optimization_barrier((own, inner, token))
        scale = (1.0 if k == 1 else 2.0) / half_width
        operands = [hamiltonian, own, inner, full[name, k - 1]]
        if k > 1:
            operands.append(full[name, k - 2])
        part = call(
            functools.partial(inside_kernel, base[name], inside, scale, scale * center_shift, k > 1),
            operands, layer, cost(PLANE, cols, 6), 12,
        )
        edge = [edges[name], halo[name, k - 1], part]
        if count == 2 * DEG - 1:
            filtered = call(
                functools.partial(last_kernel, base[name], scale),
                edge + [val[other, k]],
                jax.ShapeDtypeStruct((2 * PLANE, cols, NB), jnp.bfloat16), cost(PLANE, cols, 1), 12,
            )
            break
        kept = (layer,) if k < DEG else ()
        token, *kept = call(
            functools.partial(outside_kernel, scale),
            edge, (layer.update(dtype=jnp.bfloat16), *kept), cost(PLANE, cols, 1), 12,
        )
        val[name, k] = token
        if kept:
            full[name, k] = kept[0]
        if k < DEG:
            send(name, k)

    mine = lax.all_to_all(filtered, CHIP, 0, 0, tiled=True)
    mine = mine.reshape(chips, 2 * PLANE // chips, cols, NB)
    theirs = lax.ppermute(mine, "c", [(0, 1), (1, 0)])
    place = jnp.stack([lax.axis_index("x"), lax.axis_index("yl"), lax.axis_index("c")]).astype(jnp.int32)
    held = mine.shape[1]
    depth = held * NB
    small = pl.CostEstimate(flops=1 << 20, bytes_accessed=1 << 20, transcendentals=0)
    flops = pl.CostEstimate(flops=4 * (chips * cols) ** 2 * depth, bytes_accessed=2 << 20, transcendentals=0)

    def to_chip(away, q):
        return [(i, (i // 2 + away) % around * 2 + (i + q) % 2) for i in range(chips)]

    block = jax.ShapeDtypeStruct((chips, cols, NB), jnp.bfloat16)
    rows, *blocks = call(
        functools.partial(part_kernel, around), (place, mine, theirs),
        (jax.ShapeDtypeStruct((2 * chips * cols, depth), jnp.bfloat16), *(block,) * chips),
        flops, 16, (pltpu.VMEM((depth, 2 * chips * cols), jnp.bfloat16),), [SMEM, VMEM, VMEM],
    )
    parts = [blocks[0]]
    for away, q in SENT:
        parts.append(lax.ppermute(blocks[2 * away + q], CHIP, to_chip(away, q)))
    piece = jax.ShapeDtypeStruct((held, cols, NB), jnp.bfloat16)
    *turned, other_y = call(
        turn_kernel, (rows, shared["pair"], shared[around - 1], shared[2], shared[1]),
        (piece,) * around + (piece.update(shape=(around, *piece.shape)),), flops, 16,
    )
    crossed = lax.ppermute(other_y, "yl", [(0, 1), (1, 0)])
    pieces = []

    def along(away, value):
        pieces.append(lax.ppermute(value, "x", [(i, (i + away) % around) for i in range(around)]))

    for away in range(1, around):
        along(away, turned[away])
    total = call(
        margin_rows_kernel, parts,
        jax.ShapeDtypeStruct((slabs, cols // 2, 2 * cols), jnp.bfloat16), small, 12,
    )
    total = lax.all_to_all(total, ELEM, 0, 0, tiled=True)
    ways = call(part_ways_kernel, (crossed,), (piece,) * (around - 1), small, 12)
    for away in range(1, around):
        along(away, ways[away - 1])
    rotated = call(
        functools.partial(collect_kernel, around), (place, turned[0], crossed, *pieces),
        jax.ShapeDtypeStruct((2 * PLANE, cols, NB), jnp.float32), small, 12, (), [SMEM] + [VMEM] * (2 * around),
    )
    margin = call(
        functools.partial(margin_kernel, 1.0 / rows_total), (total,),
        jax.ShapeDtypeStruct((cols, cols), jnp.float32), small, 12,
    )
    return margin, jnp.swapaxes(rotated, 1, 2)


SENT = ((2, 1), (0, 1), (1, 1), (3, 1), (2, 0), (1, 0), (3, 0))


def solution(mesh):
    fine = Mesh(mesh.devices.reshape(8, 2, 4, 2, 2), ("z", "yh", "x", "yl", "c"))
    in_specs = (P(ELEM, None, None, None), P(ELEM, None, ORB), P(None, ORB))
    out_specs = (P(ORB, ELEM), P(ELEM, None, ORB))
    return jax.shard_map(whole, mesh=fine, in_specs=in_specs, out_specs=out_specs, check_vma=False)
```

```python
import functools

import jax
import jax.numpy as jnp
from jax import lax
from jax.experimental import pallas as pl
from jax.experimental.pallas import tpu as pltpu
from jax.sharding import Mesh, PartitionSpec as P


GY = 4
GZ = 4
NB = 128
DEG = 6
PLANE = GY * GZ

center_shift = 0.1
half_width = 1.25

ELEM = ("z", "yh")
ORB = ("x", "yl", "c")
CHIP = ("x", "yl")
VMEM = pl.BlockSpec(memory_space=pltpu.VMEM)
SMEM = pl.BlockSpec(memory_space=pltpu.SMEM)
PLAIN = (((1,), (0,)), ((), ()))


def product(left, right, contract):
    return lax.dot_general(left, right, contract, preferred_element_type=jnp.float32)


def inside_kernel(base, inside, scale, shift, has_previous, ham, own, inner, current, *rest):
    previous, out = rest if has_previous else (None, rest[0])

    def line(gy, carry):
        above = lax.rem(gy + GY - 1, GY) * GZ
        below = lax.rem(gy + 1, GY) * GZ
        for gz in range(GZ):
            e = gy * GZ + gz
            left_z, right_z = gy * GZ + (gz - 1) % GZ, gy * GZ + (gz + 1) % GZ
            terms = (
                (own[e], ham[base + e, 0], inner[e], ham[PLANE - base + e, 3 - inside]),
                (own[above + gz], ham[base + above + gz, 4], own[below + gz], ham[base + below + gz, 3]),
                (own[left_z], ham[base + left_z, 6], own[right_z], ham[base + right_z, 5]),
            )
            total = None
            for v0, h0, v1, h1 in terms:
                left, right = jnp.concatenate([v0, v1], axis=1), jnp.concatenate([h0, h1], axis=0)
                term = product(left, right, PLAIN)
                total = term if total is None else total + term
            total = scale * total - shift * current[e].astype(jnp.float32)
            if has_previous:
                total = total - previous[e].astype(jnp.float32)
            out[e] = total
        return carry

    lax.fori_loop(0, GY, line, 0)


def edges_kernel(ham, edge_a, edge_b):
    def line(gy, carry):
        for gz in range(GZ):
            e = gy * GZ + gz
            edge_a[e] = ham[e, 1].T
            edge_b[e] = ham[PLANE + e, 2].T
        return carry

    lax.fori_loop(0, GY, line, 0)


def outside_kernel(scale, edge, halo, partial, rounded, *full):
    def line(gy, carry):
        for gz in range(GZ):
            e = gy * GZ + gz
            value = partial[e] + scale * product(halo[e], edge[e], PLAIN)
            rounded[e] = value.astype(jnp.bfloat16)
            if full:
                full[0][e] = value
        return carry

    lax.fori_loop(0, GY, line, 0)


def last_kernel(base, scale, edge, halo, partial, other, filtered):
    def line(gy, carry):
        for gz in range(GZ):
            e = gy * GZ + gz
            value = partial[e] + scale * product(halo[e], edge[e], PLAIN)
            filtered[base + e] = value.astype(jnp.bfloat16)
            filtered[PLANE - base + e] = other[e]
        return carry

    lax.fori_loop(0, GY, line, 0)


def cost(elements, cols, directions):
    size = elements * cols * NB
    read = elements * NB * NB * 2 * directions
    return pl.CostEstimate(flops=2 * size * NB * directions, bytes_accessed=read, transcendentals=0)


def call(kernel, operands, out_shape, estimate, limit, scratch=(), in_specs=None):
    many = isinstance(out_shape, tuple)
    return pl.pallas_call(
        kernel,
        out_shape=out_shape,
        in_specs=in_specs or [VMEM] * len(operands),
        out_specs=(VMEM,) * len(out_shape) if many else VMEM,
        scratch_shapes=scratch,
        cost_estimate=estimate,
        compiler_params=pltpu.CompilerParams(vmem_limit_bytes=limit << 20),
    )(*operands)


def part_kernel(around, place, mine, other, rows, *refs):
    outs, across = refs[:-1], refs[-1]
    chips, held, cols = mine.shape[0], mine.shape[1], mine.shape[2]

    def fill(parity, source):
        for t in range(chips):
            for el in range(held):
                rows[pl.ds((2 * t + parity) * cols, cols), pl.ds(el * NB, NB)] = source[t, el]

    @pl.when(place[2] == 0)
    def _():
        fill(0, mine)
        fill(1, other)

    @pl.when(place[2] != 0)
    def _():
        fill(1, mine)
        fill(0, other)

    for t in range(chips):
        for el in range(held):
            across[pl.ds(el * NB, NB), pl.ds(t * NB, NB)] = rows[pl.ds(t * NB, NB), pl.ds(el * NB, NB)].T
    for away in range(around):
        line = lax.rem(place[0] + away, around) * 2
        left = []
        for q in range(2):
            chip = line + (place[1] if q == 0 else 1 - place[1])
            left.append(rows[pl.ds(pl.multiple_of((2 * chip + place[2]) * cols, cols), cols), :])
        part = product(jnp.concatenate(left, axis=0), across[...], PLAIN).astype(jnp.bfloat16)
        for q in range(2):
            for t in range(chips):
                outs[2 * away + q][t] = part[q * cols : (q + 1) * cols, t * NB : (t + 1) * NB]


def turn_kernel(rows, ritz, ritz_next, ritz_far, ritz_back, *outs):
    held, cols = outs[0].shape[0], outs[0].shape[1]
    for away, source in enumerate((ritz, ritz_next, ritz_far, ritz_back)):
        turned = product(source[...].reshape(2 * cols, -1), rows[...], PLAIN).astype(jnp.bfloat16)
        for el in range(held):
            outs[away][el] = turned[:cols, el * NB : (el + 1) * NB]
            outs[4][away, el] = turned[cols:, el * NB : (el + 1) * NB]


def part_ways_kernel(crossed, *outs):
    for away, out in enumerate(outs):
        out[...] = crossed[away + 1]


def collect_line(around, index, place):
    q, away = index // around, index % around
    return lax.rem(place[0] + around - away, around) * 2 + place[1] + q - 2 * q * place[1]


def collect_kernel(around, place, here, crossed, *refs):
    pieces, out = refs[:-1], refs[-1]
    for index in range(2 * around):
        q, away = index // around, index % around

        @pl.when(pl.program_id(0) == index)
        def _():
            if away:
                piece = pieces[q * (around - 1) + away - 1][...]
            else:
                piece = crossed[0] if q else here[...]
            out[...] = piece.astype(jnp.float32)


def margin_rows_kernel(*refs):
    pieces, out = refs[:-1], refs[-1]
    cols = out.shape[2] // 2
    half = cols // 2
    for t in range(len(pieces)):
        total = pieces[0][t].astype(jnp.float32)
        for piece in pieces[1:]:
            total = total + piece[t].astype(jnp.float32)
        for core in range(2):
            block = total[:, core * cols : (core + 1) * cols]
            out[2 * t + core] = jnp.concatenate([block[:half], block[half:]], axis=1).astype(jnp.bfloat16)


def margin_kernel(scale, got, out):
    total = got[0].astype(jnp.float32)
    for s in range(1, got.shape[0]):
        total = total + got[s].astype(jnp.float32)
    total = total * scale
    half, cols = got.shape[1], out.shape[1]
    out[0:half, :] = total[:, :cols]
    out[half : 2 * half, :] = total[:, cols:]


def whole(hamiltonian, start, ritz):
    slabs = lax.axis_size("z") * lax.axis_size("yh")
    chips = lax.axis_size("x") * lax.axis_size("yl")
    around = lax.axis_size("x")
    rows_total = float(slabs * hamiltonian.shape[0] * NB)
    cols = start.shape[2]
    layer = jax.ShapeDtypeStruct((PLANE, cols, NB), jnp.float32)
    up = [(i, (i + 1) % slabs) for i in range(slabs)]
    down = [((i + 1) % slabs, i) for i in range(slabs)]
    begin = jnp.swapaxes(start, 1, 2)
    first = begin[PLANE:]
    begin, _ = lax.optimization_barrier((begin, first))
    val = {("a", 0): begin[:PLANE], ("b", 0): first}
    full = dict(val)
    base = {"a": 0, "b": PLANE}
    halo = {}

    def send(name, k):
        if name == "a":
            halo["b", k] = lax.ppermute(val["a", k], ELEM, down)
        else:
            halo["a", k] = lax.ppermute(val["b", k], ELEM, up)

    shared = {}
    source = jnp.swapaxes(ritz, 0, 1)
    across = lax.ppermute(source, "yl", [(0, 1), (1, 0)])
    send("b", 0)
    send("a", 0)
    shared["pair"] = jnp.stack([source, across])
    for shift in (1, around - 1, 2):
        shared[shift] = lax.ppermute(shared["pair"], "x", [(i, (i + shift) % around) for i in range(around)])

    order = []
    for k in range(1, DEG + 1):
        order += [("a", k), ("b", k)] if k % 2 else [("b", k), ("a", k)]
    token = None
    blocks = jax.ShapeDtypeStruct((PLANE, NB, NB), jnp.bfloat16)
    edges = call(edges_kernel, (hamiltonian,), (blocks, blocks), cost(PLANE, cols, 2), 12)
    edges = dict(zip("ab", edges))
    for count, (name, k) in enumerate(order):
        other = "b" if name == "a" else "a"
        inside = 2 if name == "a" else 1
        own, inner = val[name, k - 1], val[other, k - 1]
        if token is not None:
            own, inner, _ = lax.optimization_barrier((own, inner, token))
        scale = (1.0 if k == 1 else 2.0) / half_width
        operands = [hamiltonian, own, inner, full[name, k - 1]]
        if k > 1:
            operands.append(full[name, k - 2])
        part = call(
            functools.partial(inside_kernel, base[name], inside, scale, scale * center_shift, k > 1),
            operands, layer, cost(PLANE, cols, 6), 12,
        )
        edge = [edges[name], halo[name, k - 1], part]
        if count == 2 * DEG - 1:
            filtered = call(
                functools.partial(last_kernel, base[name], scale),
                edge + [val[other, k]],
                jax.ShapeDtypeStruct((2 * PLANE, cols, NB), jnp.bfloat16), cost(PLANE, cols, 1), 12,
            )
            break
        kept = (layer,) if k < DEG else ()
        token, *kept = call(
            functools.partial(outside_kernel, scale),
            edge, (layer.update(dtype=jnp.bfloat16), *kept), cost(PLANE, cols, 1), 12,
        )
        val[name, k] = token
        if kept:
            full[name, k] = kept[0]
        if k < DEG:
            send(name, k)

    mine = lax.all_to_all(filtered, CHIP, 0, 0, tiled=True)
    mine = mine.reshape(chips, 2 * PLANE // chips, cols, NB)
    theirs = lax.ppermute(mine, "c", [(0, 1), (1, 0)])
    place = jnp.stack([lax.axis_index("x"), lax.axis_index("yl"), lax.axis_index("c")]).astype(jnp.int32)
    held = mine.shape[1]
    depth = held * NB
    small = pl.CostEstimate(flops=1 << 20, bytes_accessed=1 << 20, transcendentals=0)
    flops = pl.CostEstimate(flops=4 * (chips * cols) ** 2 * depth, bytes_accessed=2 << 20, transcendentals=0)

    def to_chip(away, q):
        return [(i, (i // 2 + away) % around * 2 + (i + q) % 2) for i in range(chips)]

    block = jax.ShapeDtypeStruct((chips, cols, NB), jnp.bfloat16)
    rows, *blocks = call(
        functools.partial(part_kernel, around), (place, mine, theirs),
        (jax.ShapeDtypeStruct((2 * chips * cols, depth), jnp.bfloat16), *(block,) * chips),
        flops, 16, (pltpu.VMEM((depth, 2 * chips * cols), jnp.bfloat16),), [SMEM, VMEM, VMEM],
    )
    parts = [blocks[0]]
    for away, q in SENT:
        parts.append(lax.ppermute(blocks[2 * away + q], CHIP, to_chip(away, q)))
    piece = jax.ShapeDtypeStruct((held, cols, NB), jnp.bfloat16)
    *turned, other_y = call(
        turn_kernel, (rows, shared["pair"], shared[around - 1], shared[2], shared[1]),
        (piece,) * around + (piece.update(shape=(around, *piece.shape)),), flops, 16,
    )
    crossed = lax.ppermute(other_y, "yl", [(0, 1), (1, 0)])
    pieces = []

    def along(away, value):
        pieces.append(lax.ppermute(value, "x", [(i, (i + away) % around) for i in range(around)]))

    for away in range(1, around):
        along(away, turned[away])
    total = call(
        margin_rows_kernel, parts,
        jax.ShapeDtypeStruct((slabs, cols // 2, 2 * cols), jnp.bfloat16), small, 12,
    )
    total = lax.all_to_all(total, ELEM, 0, 0, tiled=True)
    ways = call(part_ways_kernel, (crossed,), (piece,) * (around - 1), small, 12)
    for away in range(1, around):
        along(away, ways[away - 1])
    rotated = pl.pallas_call(
        functools.partial(collect_kernel, around),
        grid_spec=pltpu.PrefetchScalarGridSpec(
            num_scalar_prefetch=1,
            grid=(chips,),
            in_specs=[VMEM] * (2 * around),
            out_specs=pl.BlockSpec((held, cols, NB), lambda i, place: (collect_line(around, i, place), 0, 0)),
        ),
        out_shape=jax.ShapeDtypeStruct((2 * PLANE, cols, NB), jnp.float32),
        cost_estimate=small,
        compiler_params=pltpu.CompilerParams(vmem_limit_bytes=12 << 20),
        name="collect",
    )(place, turned[0], crossed, *pieces)
    margin = call(
        functools.partial(margin_kernel, 1.0 / rows_total), (total,),
        jax.ShapeDtypeStruct((cols, cols), jnp.float32), small, 12,
    )
    return margin, jnp.swapaxes(rotated, 1, 2)


SENT = ((2, 1), (0, 1), (1, 1), (3, 1), (2, 0), (1, 0), (3, 0))


def solution(mesh):
    fine = Mesh(mesh.devices.reshape(8, 2, 4, 2, 2), ("z", "yh", "x", "yl", "c"))
    in_specs = (P(ELEM, None, None, None), P(ELEM, None, ORB), P(None, ORB))
    out_specs = (P(ORB, ELEM), P(ELEM, None, ORB))
    return jax.shard_map(whole, mesh=fine, in_specs=in_specs, out_specs=out_specs, check_vma=False)
```

```python
import functools

import jax
import jax.numpy as jnp
from jax import lax
from jax.experimental import pallas as pl
from jax.experimental.pallas import tpu as pltpu
from jax.sharding import Mesh, PartitionSpec as P


GY = 4
GZ = 4
NB = 128
DEG = 6
PLANE = GY * GZ

center_shift = 0.1
half_width = 1.25

ELEM = ("z", "yh")
ORB = ("x", "yl", "c")
CHIP = ("x", "yl")
VMEM = pl.BlockSpec(memory_space=pltpu.VMEM)
SMEM = pl.BlockSpec(memory_space=pltpu.SMEM)
PLAIN = (((1,), (0,)), ((), ()))


def product(left, right, contract):
    return lax.dot_general(left, right, contract, preferred_element_type=jnp.float32)


def inside_kernel(base, inside, scale, shift, has_previous, ham, own, inner, current, *rest):
    previous, out = rest if has_previous else (None, rest[0])

    def line(gy, carry):
        above = lax.rem(gy + GY - 1, GY) * GZ
        below = lax.rem(gy + 1, GY) * GZ
        for gz in range(GZ):
            e = gy * GZ + gz
            left_z, right_z = gy * GZ + (gz - 1) % GZ, gy * GZ + (gz + 1) % GZ
            terms = (
                (own[e], ham[base + e, 0], inner[e], ham[PLANE - base + e, 3 - inside]),
                (own[above + gz], ham[base + above + gz, 4], own[below + gz], ham[base + below + gz, 3]),
                (own[left_z], ham[base + left_z, 6], own[right_z], ham[base + right_z, 5]),
            )
            total = None
            for v0, h0, v1, h1 in terms:
                left, right = jnp.concatenate([v0, v1], axis=1), jnp.concatenate([h0, h1], axis=0)
                term = product(left, right, PLAIN)
                total = term if total is None else total + term
            total = scale * total - shift * current[e].astype(jnp.float32)
            if has_previous:
                total = total - previous[e].astype(jnp.float32)
            out[e] = total
        return carry

    lax.fori_loop(0, GY, line, 0)


def edges_kernel(ham, edge_a, edge_b):
    def line(gy, carry):
        for gz in range(GZ):
            e = gy * GZ + gz
            edge_a[e] = ham[e, 1].T
            edge_b[e] = ham[PLANE + e, 2].T
        return carry

    lax.fori_loop(0, GY, line, 0)


def outside_kernel(scale, edge, halo, partial, rounded, *full):
    def line(gy, carry):
        for gz in range(GZ):
            e = gy * GZ + gz
            value = partial[e] + scale * product(halo[e], edge[e], PLAIN)
            rounded[e] = value.astype(jnp.bfloat16)
            if full:
                full[0][e] = value
        return carry

    lax.fori_loop(0, GY, line, 0)


def last_kernel(base, scale, edge, halo, partial, other, filtered):
    def line(gy, carry):
        for gz in range(GZ):
            e = gy * GZ + gz
            value = partial[e] + scale * product(halo[e], edge[e], PLAIN)
            filtered[base + e] = value.astype(jnp.bfloat16)
            filtered[PLANE - base + e] = other[e]
        return carry

    lax.fori_loop(0, GY, line, 0)


def cost(elements, cols, directions):
    size = elements * cols * NB
    read = elements * NB * NB * 2 * directions
    return pl.CostEstimate(flops=2 * size * NB * directions, bytes_accessed=read, transcendentals=0)


def call(kernel, operands, out_shape, estimate, limit, scratch=(), in_specs=None):
    many = isinstance(out_shape, tuple)
    return pl.pallas_call(
        kernel,
        out_shape=out_shape,
        in_specs=in_specs or [VMEM] * len(operands),
        out_specs=(VMEM,) * len(out_shape) if many else VMEM,
        scratch_shapes=scratch,
        cost_estimate=estimate,
        compiler_params=pltpu.CompilerParams(vmem_limit_bytes=limit << 20),
    )(*operands)


def part_kernel(around, place, mine, other, rows, *refs):
    outs, across = refs[:-1], refs[-1]
    chips, held, cols = mine.shape[0], mine.shape[1], mine.shape[2]

    def fill(parity, source):
        for t in range(chips):
            for el in range(held):
                rows[pl.ds((2 * t + parity) * cols, cols), pl.ds(el * NB, NB)] = source[t, el]

    @pl.when(place[2] == 0)
    def _():
        fill(0, mine)
        fill(1, other)

    @pl.when(place[2] != 0)
    def _():
        fill(1, mine)
        fill(0, other)

    for t in range(chips):
        for el in range(held):
            across[pl.ds(el * NB, NB), pl.ds(t * NB, NB)] = rows[pl.ds(t * NB, NB), pl.ds(el * NB, NB)].T
    for away in range(around):
        line = lax.rem(place[0] + away, around) * 2
        left = []
        for q in range(2):
            chip = line + (place[1] if q == 0 else 1 - place[1])
            left.append(rows[pl.ds(pl.multiple_of((2 * chip + place[2]) * cols, cols), cols), :])
        part = product(jnp.concatenate(left, axis=0), across[...], PLAIN).astype(jnp.bfloat16)
        for q in range(2):
            for t in range(chips):
                outs[2 * away + q][t] = part[q * cols : (q + 1) * cols, t * NB : (t + 1) * NB]


def turn_kernel(rows, ritz, ritz_next, ritz_far, ritz_back, *outs):
    held, cols = outs[0].shape[0], outs[0].shape[1]
    for away, source in enumerate((ritz, ritz_next, ritz_far, ritz_back)):
        turned = product(source[...].reshape(2 * cols, -1), rows[...], PLAIN).astype(jnp.bfloat16)
        for el in range(held):
            outs[away][el] = turned[:cols, el * NB : (el + 1) * NB]
            outs[4][away, el] = turned[cols:, el * NB : (el + 1) * NB]


def join_kernel(crossed, *refs):
    count = len(refs) // 2
    for away in range(count):
        refs[count + away][0] = refs[away][...]
        refs[count + away][1] = crossed[away + 1]


def collect_kernel(around, place, here, crossed, *refs):
    pieces, out = refs[:-1], refs[-1]
    held = here.shape[0]
    for q in range(2):
        near = place[1] if q == 0 else 1 - place[1]
        for away in range(around):
            line = lax.rem(place[0] + around - away, around) * 2 + near
            for el in range(held):
                if away:
                    piece = pieces[away - 1][q, el]
                else:
                    piece = crossed[0, el] if q else here[el]
                out[line * held + el] = piece.astype(jnp.float32)


def margin_rows_kernel(*refs):
    pieces, out = refs[:-1], refs[-1]
    cols = out.shape[2] // 2
    half = cols // 2
    for t in range(len(pieces)):
        total = pieces[0][t].astype(jnp.float32)
        for piece in pieces[1:]:
            total = total + piece[t].astype(jnp.float32)
        for core in range(2):
            block = total[:, core * cols : (core + 1) * cols]
            out[2 * t + core] = jnp.concatenate([block[:half], block[half:]], axis=1).astype(jnp.bfloat16)


def margin_kernel(scale, got, out):
    total = got[0].astype(jnp.float32)
    for s in range(1, got.shape[0]):
        total = total + got[s].astype(jnp.float32)
    total = total * scale
    half, cols = got.shape[1], out.shape[1]
    out[0:half, :] = total[:, :cols]
    out[half : 2 * half, :] = total[:, cols:]


def whole(hamiltonian, start, ritz):
    slabs = lax.axis_size("z") * lax.axis_size("yh")
    chips = lax.axis_size("x") * lax.axis_size("yl")
    around = lax.axis_size("x")
    rows_total = float(slabs * hamiltonian.shape[0] * NB)
    cols = start.shape[2]
    layer = jax.ShapeDtypeStruct((PLANE, cols, NB), jnp.float32)
    up = [(i, (i + 1) % slabs) for i in range(slabs)]
    down = [((i + 1) % slabs, i) for i in range(slabs)]
    begin = jnp.swapaxes(start, 1, 2)
    val = {("a", 0): begin[:PLANE], ("b", 0): begin[PLANE:]}
    full = dict(val)
    base = {"a": 0, "b": PLANE}
    halo = {}

    def send(name, k):
        if name == "a":
            halo["b", k] = lax.ppermute(val["a", k], ELEM, down)
        else:
            halo["a", k] = lax.ppermute(val["b", k], ELEM, up)

    shared = {}
    source = jnp.swapaxes(ritz, 0, 1)
    across = lax.ppermute(source, "yl", [(0, 1), (1, 0)])
    send("b", 0)
    send("a", 0)
    shared["pair"] = jnp.stack([source, across])
    for shift in (1, around - 1, 2):
        shared[shift] = lax.ppermute(shared["pair"], "x", [(i, (i + shift) % around) for i in range(around)])

    order = []
    for k in range(1, DEG + 1):
        order += [("a", k), ("b", k)] if k % 2 else [("b", k), ("a", k)]
    token = None
    blocks = jax.ShapeDtypeStruct((PLANE, NB, NB), jnp.bfloat16)
    edges = call(edges_kernel, (hamiltonian,), (blocks, blocks), cost(PLANE, cols, 2), 12)
    edges = dict(zip("ab", edges))
    for count, (name, k) in enumerate(order):
        other = "b" if name == "a" else "a"
        inside = 2 if name == "a" else 1
        own, inner = val[name, k - 1], val[other, k - 1]
        if token is not None:
            own, inner, _ = lax.optimization_barrier((own, inner, token))
        scale = (1.0 if k == 1 else 2.0) / half_width
        operands = [hamiltonian, own, inner, full[name, k - 1]]
        if k > 1:
            operands.append(full[name, k - 2])
        part = call(
            functools.partial(inside_kernel, base[name], inside, scale, scale * center_shift, k > 1),
            operands, layer, cost(PLANE, cols, 6), 12,
        )
        edge = [edges[name], halo[name, k - 1], part]
        if count == 2 * DEG - 1:
            filtered = call(
                functools.partial(last_kernel, base[name], scale),
                edge + [val[other, k]],
                jax.ShapeDtypeStruct((2 * PLANE, cols, NB), jnp.bfloat16), cost(PLANE, cols, 1), 12,
            )
            break
        kept = (layer,) if k < DEG else ()
        token, *kept = call(
            functools.partial(outside_kernel, scale),
            edge, (layer.update(dtype=jnp.bfloat16), *kept), cost(PLANE, cols, 1), 12,
        )
        val[name, k] = token
        if kept:
            full[name, k] = kept[0]
        if k < DEG:
            send(name, k)

    mine = lax.all_to_all(filtered, CHIP, 0, 0, tiled=True)
    mine = mine.reshape(chips, 2 * PLANE // chips, cols, NB)
    theirs = lax.ppermute(mine, "c", [(0, 1), (1, 0)])
    place = jnp.stack([lax.axis_index("x"), lax.axis_index("yl"), lax.axis_index("c")]).astype(jnp.int32)
    held = mine.shape[1]
    depth = held * NB
    small = pl.CostEstimate(flops=1 << 20, bytes_accessed=1 << 20, transcendentals=0)
    flops = pl.CostEstimate(flops=4 * (chips * cols) ** 2 * depth, bytes_accessed=2 << 20, transcendentals=0)

    def to_chip(away, q):
        return [(i, (i // 2 + away) % around * 2 + (i + q) % 2) for i in range(chips)]

    block = jax.ShapeDtypeStruct((chips, cols, NB), jnp.bfloat16)
    rows, *blocks = call(
        functools.partial(part_kernel, around), (place, mine, theirs),
        (jax.ShapeDtypeStruct((2 * chips * cols, depth), jnp.bfloat16), *(block,) * chips),
        flops, 16, (pltpu.VMEM((depth, 2 * chips * cols), jnp.bfloat16),), [SMEM, VMEM, VMEM],
    )
    parts = [blocks[0]]
    for away, q in SENT:
        parts.append(lax.ppermute(blocks[2 * away + q], CHIP, to_chip(away, q)))
    piece = jax.ShapeDtypeStruct((held, cols, NB), jnp.bfloat16)
    *turned, other_y = call(
        turn_kernel, (rows, shared["pair"], shared[around - 1], shared[2], shared[1]),
        (piece,) * around + (piece.update(shape=(around, *piece.shape)),), flops, 16,
    )
    crossed = lax.ppermute(other_y, "yl", [(0, 1), (1, 0)])
    pieces = []

    def along(away, value):
        pieces.append(lax.ppermute(value, "x", [(i, (i + away) % around) for i in range(around)]))

    total = call(
        margin_rows_kernel, parts,
        jax.ShapeDtypeStruct((slabs, cols // 2, 2 * cols), jnp.bfloat16), small, 12,
    )
    total = lax.all_to_all(total, ELEM, 0, 0, tiled=True)
    joined = call(
        join_kernel, (crossed, *turned[1:]),
        (piece.update(shape=(2, *piece.shape)),) * (around - 1), small, 12,
    )
    for away in range(1, around):
        along(away, joined[away - 1])
    rotated = call(
        functools.partial(collect_kernel, around), (place, turned[0], crossed, *pieces),
        jax.ShapeDtypeStruct((2 * PLANE, cols, NB), jnp.float32), small, 12, (), [SMEM] + [VMEM] * (around + 1),
    )
    margin = call(
        functools.partial(margin_kernel, 1.0 / rows_total), (total,),
        jax.ShapeDtypeStruct((cols, cols), jnp.float32), small, 12,
    )
    return margin, jnp.swapaxes(rotated, 1, 2)


SENT = ((2, 1), (0, 1), (1, 1), (3, 1), (2, 0), (1, 0), (3, 0))


def solution(mesh):
    fine = Mesh(mesh.devices.reshape(8, 2, 4, 2, 2), ("z", "yh", "x", "yl", "c"))
    in_specs = (P(ELEM, None, None, None), P(ELEM, None, ORB), P(None, ORB))
    out_specs = (P(ORB, ELEM), P(ELEM, None, ORB))
    return jax.shard_map(whole, mesh=fine, in_specs=in_specs, out_specs=out_specs, check_vma=False)
```
